128 devices in a mesh: gx: 4 (over z_lo, core), gy: 8 (over z_hi, x), gz: 4 (over y).
Axes of the slice: x: 4, y: 4, z: 4 (z_hi: 2, z_lo: 2; z = z_hi * 2 + z_lo), core: 2. Of those that a mesh axis runs over, the one named last changes fastest.
Arguments:
- velocity: float32 [6, 2097152], P(None, ('gx', 'gy', 'gz')), may hold values from -6 to 6
- positions: float32 [3, 2097152], P(None, ('gx', 'gy', 'gz')), may hold values from 0 to 100
- inverse_mass: float32 [2097152], P(('gx', 'gy', 'gz')), may hold values from 0.2 to 2
- inverse_inertia: float32 [3, 2097152], P(None, ('gx', 'gy', 'gz')), may hold values from 0.5 to 5
- normals: float32 [3, 8, 2097152], P(None, None, ('gx', 'gy', 'gz')), may hold values from -1 to 1
- lever_own: float32 [3, 8, 2097152], P(None, None, ('gx', 'gy', 'gz')), may hold values from -0.5 to 0.5
- lever_other: float32 [3, 8, 2097152], P(None, None, ('gx', 'gy', 'gz')), may hold values from -0.5 to 0.5
- speed_bias: float32 [8, 2097152], P(None, ('gx', 'gy', 'gz')), may hold values from -0.6 to 0.2
- contact_mass: float32 [8, 2097152], P(None, ('gx', 'gy', 'gz')), may hold values from 0.1 to 1
- partner_block: int32 [8, 16384], P(None, ('gx', 'gy', 'gz')), may hold values from 0 to 367
- partner_lane: int32 [8, 2097152], P(None, ('gx', 'gy', 'gz')), may hold values from 0 to 127
- slot_counts: int32 [2097152], P(('gx', 'gy', 'gz')), may hold values from 1 to 8
- ghost_blocks: int32 [6, 5120], P(None, ('gx', 'gy', 'gz')), may hold values from 0 to 127
Outputs:
- velocity_out: float32 [6, 2097152], P(None, ('gx', 'gy', 'gz'))
- positions_out: float32 [3, 2097152], P(None, ('gx', 'gy', 'gz'))
The draws below stay inside these ranges and needn't reach their ends.
Inputs may be any that keep to these rules, and one draw needn't show every extreme that they name: `partner_block`: column j belongs to block j; blocks below 128 are the tile's own; the rest are ghost blocks, 40 to a region, region by region as in the reference program. `slot_counts`: slots at or beyond a body's count are padding. `ghost_blocks`: block numbers within the sending tile.
All inputs are finite; a program needn't handle non-finite values.
Results may differ from the reference program's by a relative error of at most 0.0001.
Values sent between devices are 32-bit elements; how exact they have to be, the bound alone decides.
A program may use at most 128 MiB of HBM per device.

```python
import math
import jax
import jax.numpy as jnp
from jax import lax

BLOCK = 128
BLK_DEV = 128
K = 8
GHOST = 40
ITERS = 3
BODIES = 2097152
BLOCKS_ALL = 16384
GHOST_ALL = 5120
N_GX = 4
N_GY = 8
N_GZ = 4
DEVICES = 128


def set_ends(result, stream_key, least, largest):
    extent = result.shape
    spot = [jax.random.randint(jax.random.fold_in(stream_key, axis), (), 0, extent[axis]) for axis in range(len(extent))]
    result = result.at[tuple(spot)].set(least)
    longest = extent.index(max(extent))
    spot[longest] = (spot[longest] + 1) % extent[longest]
    return result.at[tuple(spot)].set(largest)


def level_of(stream_key, extent, cuts, smallest, largest):
    factor_of = 1.0
    for position, parts in cuts:
        draws = jax.random.uniform(jax.random.fold_in(jax.random.fold_in(stream_key, 6), position), (parts,), jnp.float32, smallest / len(cuts), largest / len(cuts))
        factor_of = factor_of * jnp.repeat(jnp.exp(draws), extent[position] // parts).reshape((-1,) + (1,) * (len(extent) - 1 - position))
    return factor_of


def gaussian(stream_key, extent, scale, bound, cuts=(), dtype=jnp.bfloat16):
    values = jax.random.normal(stream_key, extent, jnp.float32) * scale
    if len(cuts) > 0:
        values = level_of(stream_key, extent, cuts, -0.22, 0.18) * values
    return jnp.clip(values, min=-bound, max=bound).astype(dtype)


def setup_inputs(seed: int = 0) -> dict:
    streams_of = jax.random.split(jax.random.key(seed), 14)
    velocity = gaussian(streams_of[0], (6, BODIES), 1.0, 6.0, ((1, 128),), jnp.float32)
    positions = jnp.clip(100.0 * jax.random.uniform(streams_of[1], (3, BODIES), jnp.float32) ** level_of(streams_of[1], (3, BODIES), ((1, 128),), -0.2, 0.2), 0.0, 100.0)
    inverse_mass = jnp.clip(jnp.exp(math.log(2.0) - 2.3025851 * jax.random.uniform(streams_of[2], (BODIES,), jnp.float32) ** level_of(streams_of[2], (BODIES,), ((0, 128),), -0.2, 0.2)), 0.2, 2.0)
    inverse_inertia = jnp.clip(jnp.exp(math.log(5.0) - 2.3025851 * jax.random.uniform(streams_of[3], (3, BODIES), jnp.float32) ** level_of(streams_of[3], (3, BODIES), ((1, 128),), -0.2, 0.2)), 0.5, 5.0)
    normals = jnp.clip(jax.random.uniform(streams_of[4], (3, K, BODIES), jnp.float32, -1.0, 1.0) * level_of(streams_of[4], (3, K, BODIES), ((2, 128),), -0.4, 0.0), -1.0, 1.0)
    lever_own = jnp.clip(jax.random.uniform(streams_of[5], (3, K, BODIES), jnp.float32, -0.5, 0.5) * level_of(streams_of[5], (3, K, BODIES), ((2, 128),), -0.4, 0.0), -0.5, 0.5)
    lever_other = jnp.clip(jax.random.uniform(streams_of[6], (3, K, BODIES), jnp.float32, -0.5, 0.5) * level_of(streams_of[6], (3, K, BODIES), ((2, 128),), -0.4, 0.0), -0.5, 0.5)
    speed_bias = jnp.clip(-0.6 + 0.8 * jax.random.uniform(streams_of[7], (K, BODIES), jnp.float32) ** level_of(streams_of[7], (K, BODIES), ((1, 128),), -0.2, 0.2), -0.6, 0.2)
    contact_mass = jnp.clip(jnp.exp(math.log(1.0) - 2.3025851 * jax.random.uniform(streams_of[8], (K, BODIES), jnp.float32) ** level_of(streams_of[8], (K, BODIES), ((1, 128),), -0.2, 0.2)), 0.1, 1.0)
    partner_block = set_ends(jax.random.randint(streams_of[9], (K, BLOCKS_ALL), 0, BLK_DEV + 6 * GHOST), jax.random.fold_in(streams_of[9], 1), 0, (BLK_DEV + 6 * GHOST) - 1).astype(jnp.int32)
    partner_lane = set_ends(jax.random.randint(streams_of[10], (K, BODIES), 0, BLOCK), jax.random.fold_in(streams_of[10], 1), 0, BLOCK - 1).astype(jnp.int32)
    slot_counts = set_ends(jax.random.randint(streams_of[11], (BODIES,), 1, K + 1), jax.random.fold_in(streams_of[11], 1), 1, K).astype(jnp.int32)
    ghost_blocks = set_ends(jax.random.randint(streams_of[12], (6, GHOST_ALL), 0, BLK_DEV), jax.random.fold_in(streams_of[12], 1), 0, BLK_DEV - 1).astype(jnp.int32)
    return {"velocity": velocity, "positions": positions, "inverse_mass": inverse_mass, "inverse_inertia": inverse_inertia, "normals": normals, "lever_own": lever_own, "lever_other": lever_other, "speed_bias": speed_bias, "contact_mass": contact_mass, "partner_block": partner_block, "partner_lane": partner_lane, "slot_counts": slot_counts, "ghost_blocks": ghost_blocks}


relaxation = 0.25
time_step = 1.0 / 60.0


def cross_product(first, second):
    return jnp.stack([first[1] * second[2] - first[2] * second[1],
                      first[2] * second[0] - first[0] * second[2],
                      first[0] * second[1] - first[1] * second[0]])


def face_buffers(velocity, ghost_blocks):
    blocks = velocity.shape[1] // BLOCK
    pieces = jnp.take(velocity.reshape(6, blocks, BLOCK), ghost_blocks, axis=1)
    return [pieces[:, number].reshape(6, -1) for number in range(6)]


def contact_sweep(velocity, ghosts, impulse, normals, cross_own, cross_other, speed_bias, contact_mass, partner, live_slot, inverse_mass, inverse_inertia):
    extended = jnp.concatenate([velocity, ghosts], axis=1)
    partner_vel = jnp.take(extended, partner, axis=1)
    approach = (jnp.sum(normals * partner_vel[:3], 0) + jnp.sum(cross_other * partner_vel[3:], 0)
                - jnp.sum(normals * velocity[:3, None, :], 0) - jnp.sum(cross_own * velocity[3:, None, :], 0))
    updated = jnp.maximum(impulse - relaxation * contact_mass * (approach + speed_bias), 0.0) * live_slot
    change = updated - impulse
    linear = velocity[:3] - inverse_mass[None, :] * jnp.sum(change[None] * normals, axis=1)
    angular = velocity[3:] - inverse_inertia * jnp.sum(change[None] * cross_own, axis=1)
    return jnp.concatenate([linear, angular], axis=0), updated


def per_device(array):
    shaped = array.reshape(array.shape[:-1] + (DEVICES, -1))
    return jnp.moveaxis(shaped, -2, 0)


def on_grid(array):
    return array.reshape((N_GX, N_GY, N_GZ) + array.shape[1:])


def reference(velocity, positions, inverse_mass, inverse_inertia, normals, lever_own, lever_other, speed_bias, contact_mass, partner_block, partner_lane, slot_counts, ghost_blocks):
    cross_own = cross_product(lever_own, normals)
    cross_other = cross_product(lever_other, normals)
    block_full = jnp.repeat(partner_block.astype(jnp.int32), BLOCK, axis=1)
    partner = (block_full * BLOCK + partner_lane.astype(jnp.int32)).astype(jnp.int32)
    live_slot = (lax.broadcasted_iota(jnp.int32, partner.shape, 0) < slot_counts[None, :].astype(jnp.int32)).astype(jnp.float32)
    bundle = tuple(per_device(item) for item in (normals, cross_own, cross_other, speed_bias, contact_mass, partner, live_slot, inverse_mass, inverse_inertia))
    dev_vel = per_device(velocity)
    dev_ghost = per_device(ghost_blocks)
    dev_impulse = jnp.zeros((DEVICES, K, BLK_DEV * BLOCK), jnp.float32)
    for iteration in range(ITERS):
        sends = jax.vmap(face_buffers)(dev_vel, dev_ghost)
        regions = []
        for axis_number in range(3):
            lower = jnp.roll(on_grid(sends[2 * axis_number + 1]), 1, axis=axis_number)
            upper = jnp.roll(on_grid(sends[2 * axis_number]), -1, axis=axis_number)
            regions.append(lower.reshape((DEVICES,) + lower.shape[3:]))
            regions.append(upper.reshape((DEVICES,) + upper.shape[3:]))
        ghosts = jnp.concatenate(regions, axis=2)

        def sweep_device(items):
            return contact_sweep(*items)

        dev_vel, dev_impulse = lax.map(sweep_device, (dev_vel, ghosts, dev_impulse) + bundle)
    velocity_out = jnp.moveaxis(dev_vel, 0, 1).reshape(6, -1)
    positions_out = positions + time_step * velocity_out[:3]
    return velocity_out, positions_out
```

```python
import functools

import jax
import jax.numpy as jnp
from jax import lax
from jax.experimental import pallas as pl
from jax.experimental.pallas import tpu as pltpu
from jax.sharding import PartitionSpec as P

BLOCK = 128
BLK = 128
K = 8
GHOST = 40
ITERS = 3
EXT = BLK + 6 * GHOST
FACE_ROWS = GHOST * 6
RELAXATION = 0.25
TIME_STEP = 1.0 / 60.0
MESH = pl.DeviceIdType.MESH
UNROLL = 4
FACE_OF_REGION = (1, 0, 3, 2, 5, 4)


def slot_sums(terms):
    sub = lax.broadcasted_iota(jnp.int32, (8, BLOCK), 0)

    def merge(first, second, bit):
        low = (sub & bit) == 0
        if second is None:
            return first + pltpu.roll(first, bit, 0)
        if bit == 4:
            return jnp.where(low, first, second) + pltpu.roll(jnp.where(low, second, first), 4, 0)
        up = jnp.where(low, first, second)
        other = jnp.where(low, second, first)
        return up + jnp.where(low, pltpu.roll(other, 8 - bit, 0), pltpu.roll(other, bit, 0))

    level = [merge(terms[0], terms[4], 4), merge(terms[1], terms[5], 4), merge(terms[2], None, 4), merge(terms[3], None, 4)]
    level = [merge(level[0], level[2], 2), merge(level[1], level[3], 2)]
    return merge(level[0], level[1], 1)


def kernel(
    vel_h, pos_h, im_h, ii_h, nrm_h, lo_h, lt_h, bias_h, mass_h, pb_h, lane_h, cnt_h, gb_h,
    vout, pout,
    pos, im, ii, nrm, co, ct, base, bias, mass, lane, cnt, inv, imp, vin,
    ext0, ext1, ext2, own, send, tmp, pb, gb,
    in_sem, send_sem, recv_sem,
):
    gx, gy, gz = lax.axis_index("gx"), lax.axis_index("gy"), lax.axis_index("gz")
    nx, ny, nz = lax.axis_size("gx"), lax.axis_size("gy"), lax.axis_size("gz")
    near = [
        ((gx + nx - 1) % nx, gy, gz), ((gx + 1) % nx, gy, gz),
        (gx, (gy + ny - 1) % ny, gz), (gx, (gy + 1) % ny, gz),
        (gx, gy, (gz + nz - 1) % nz), (gx, gy, (gz + 1) % nz),
    ]
    exts = [ext0, ext1, ext2]

    loads = [
        pltpu.make_async_copy(s, d, in_sem.at[i])
        for i, (s, d) in enumerate([
            (gb_h, gb), (vel_h, vin), (pb_h, pb), (nrm_h, nrm), (lo_h, co), (lt_h, ct), (bias_h, bias),
            (mass_h, mass), (cnt_h, cnt), (im_h, im), (ii_h, ii), (lane_h, lane), (pos_h, pos),
        ])
    ]
    loads[0].start()
    loads[1].start()
    barrier = pltpu.get_barrier_semaphore()
    for device in near:
        pl.semaphore_signal(barrier, inc=1, device_id=device, device_id_type=MESH)
    for load in loads[2:]:
        load.start()

    def column(b):
        return pl.ds(pl.multiple_of(b * BLOCK, BLOCK), BLOCK)

    def loop(count, body, unroll=UNROLL):
        def step(i, carry):
            for u in range(unroll):
                body(i * unroll + u, u)
            return carry
        lax.fori_loop(0, count // unroll, step, 0)

    def copies(round_number):
        made = []
        for region in range(6):
            face = FACE_OF_REGION[region]
            made.append(pltpu.make_async_remote_copy(
                src_ref=send.at[round_number, pl.ds(face * FACE_ROWS, FACE_ROWS)],
                dst_ref=exts[round_number].at[pl.ds((BLK + region * GHOST) * 6, FACE_ROWS)],
                send_sem=send_sem.at[round_number, face],
                recv_sem=recv_sem.at[round_number, face],
                device_id=near[face],
                device_id_type=MESH,
            ))
        return made

    def pack_faces(round_number):
        def body(g, u):
            for face in range(6):
                send[round_number, pl.ds(face * FACE_ROWS + g * 6, 6), :] = own[pl.ds(gb[face, g] * 8, 6), :]
        loop(GHOST, body, 4)

    loads[1].wait()

    def unpack(b, u):
        rows = vin[:, column(b)]
        own[pl.ds(pl.multiple_of(b * 8, 8), 6), :] = rows
        ext0[pl.ds(b * 6, 6), :] = rows
    loop(BLK, unpack)
    loads[0].wait()
    pack_faces(0)
    pl.semaphore_wait(barrier, 6)
    pending = copies(0)
    for copy in pending:
        copy.start()

    for load in loads[2:]:
        load.wait()

    slot_index = lax.broadcasted_iota(jnp.int32, (K, BLOCK), 0)

    def base_of(b, n, c_own, own_rows):
        total = bias[:, column(b)]
        for c in range(3):
            total = total - n[c] * own_rows(c)
            total = total - c_own[c] * own_rows(c + 3)
        base[:, column(b)] = total

    def cross(first, second):
        return [
            first[1] * second[2] - first[2] * second[1],
            first[2] * second[0] - first[0] * second[2],
            first[0] * second[1] - first[1] * second[0],
        ]

    def prepare(b, u):
        cols = column(b)
        n = [nrm[c, :, cols] for c in range(3)]
        c_own = cross([co[c, :, cols] for c in range(3)], n)
        c_other = cross([ct[c, :, cols] for c in range(3)], n)
        for c in range(3):
            co[c, :, cols] = c_own[c]
            ct[c, :, cols] = c_other[c]
        live = slot_index < jnp.broadcast_to(cnt[pl.ds(b, 1), :], (K, BLOCK))
        mass[:, cols] = jnp.where(live, RELAXATION * mass[:, cols], 0.0)
        row = pl.multiple_of(b * 8, 8)
        inv[pl.ds(row, 3), :] = jnp.broadcast_to(im[pl.ds(b, 1), :], (3, BLOCK))
        inv[pl.ds(row + 3, 3), :] = ii[:, cols]
        base_of(b, n, c_own, lambda c: jnp.broadcast_to(own[pl.ds(row + c, 1), :], (K, BLOCK)))
    loop(BLK, prepare, 2)

    for it in range(ITERS):
        ext = exts[it]
        for copy in pending:
            copy.wait()
        last = it == ITERS - 1

        def sweep(b, u):
            cols = column(b)
            stage = u * 64
            for k in range(K):
                tmp[pl.ds(stage + 8 * k, 8), :] = ext[pl.ds(pb[k, b] * 6, 8), :]
            lanes = lane[:, cols]
            n = [nrm[c, :, cols] for c in range(3)]
            c_own = [co[c, :, cols] for c in range(3)]
            total = base[:, cols]
            for c in range(6):
                rows = tmp[pl.ds(stage + c, 8, stride=8), :]
                picked = jnp.take_along_axis(rows, lanes, axis=1, mode="promise_in_bounds")
                total = total + (n[c] if c < 3 else ct[c - 3, :, cols]) * picked
            step = mass[:, cols] * total
            if it == 0:
                change = jnp.maximum(-step, 0.0)
                new = change
            else:
                old = imp[:, cols]
                new = jnp.maximum(old - step, 0.0)
                change = new - old
            if not last:
                imp[:, cols] = new
            sums = slot_sums([change * (n[c] if c < 3 else c_own[c - 3]) for c in range(6)])
            row = pl.multiple_of(b * 8, 8)
            moved = (own[pl.ds(row, 8), :] - inv[pl.ds(row, 8), :] * sums)[:6]
            if last:
                vout[:, cols] = moved
                pout[:, cols] = pos[:, cols] + TIME_STEP * moved[:3]
            else:
                own[pl.ds(row, 6), :] = moved
                exts[it + 1][pl.ds(b * 6, 6), :] = moved
        loop(BLK, sweep)

        if not last:
            pack_faces(it + 1)
            pending = copies(it + 1)
            for copy in pending:
                copy.start()

            def rebase(b, u):
                cols = column(b)
                row = pl.multiple_of(b * 8, 8)
                base_of(
                    b, [nrm[c, :, cols] for c in range(3)], [co[c, :, cols] for c in range(3)],
                    lambda c: jnp.broadcast_to(own[pl.ds(row + c, 1), :], (K, BLOCK)),
                )
            loop(BLK, rebase)


def per_device(
    velocity, positions, inverse_mass, inverse_inertia, normals, lever_own, lever_other, speed_bias, contact_mass,
    partner_block, partner_lane, slot_counts, ghost_blocks,
):
    bodies = BLK * BLOCK
    slots = pltpu.VMEM((K, bodies), jnp.float32)
    vectors = pltpu.VMEM((3, K, bodies), jnp.float32)
    table = pltpu.VMEM((EXT * 6 + 8, BLOCK), jnp.float32)
    hbm = pl.BlockSpec(memory_space=pl.ANY)
    vmem = pl.BlockSpec(memory_space=pltpu.VMEM)
    return pl.pallas_call(
        kernel,
        out_shape=(
            jax.ShapeDtypeStruct((6, bodies), jnp.float32),
            jax.ShapeDtypeStruct((3, bodies), jnp.float32),
        ),
        in_specs=[hbm] * 13,
        out_specs=(vmem, vmem),
        scratch_shapes=[
            pltpu.VMEM((3, bodies), jnp.float32),
            pltpu.VMEM((BLK, BLOCK), jnp.float32),
            pltpu.VMEM((3, bodies), jnp.float32),
            vectors, vectors, vectors,
            slots, slots, slots,
            pltpu.VMEM((K, bodies), jnp.int32),
            pltpu.VMEM((BLK, BLOCK), jnp.int32),
            pltpu.VMEM((BLK * 8, BLOCK), jnp.float32),
            slots,
            pltpu.VMEM((6, bodies), jnp.float32),
            table, table, table,
            pltpu.VMEM((BLK * 8, BLOCK), jnp.float32),
            pltpu.VMEM((ITERS, 6 * FACE_ROWS, BLOCK), jnp.float32),
            pltpu.VMEM((UNROLL * 64, BLOCK), jnp.float32),
            pltpu.SMEM((K, BLK), jnp.int32),
            pltpu.SMEM((6, GHOST), jnp.int32),
            pltpu.SemaphoreType.DMA((13,)),
            pltpu.SemaphoreType.DMA((ITERS, 6)),
            pltpu.SemaphoreType.DMA((ITERS, 6)),
        ],
        compiler_params=pltpu.CompilerParams(collective_id=0, has_side_effects=True),
    )(
        velocity, positions, inverse_mass.reshape(BLK, BLOCK), inverse_inertia, normals, lever_own, lever_other,
        speed_bias, contact_mass, partner_block, partner_lane, slot_counts.reshape(BLK, BLOCK), ghost_blocks,
    )


def solution(mesh):
    every = ("gx", "gy", "gz")
    flat, wide, deep = P(every), P(None, every), P(None, None, every)
    return jax.shard_map(
        per_device,
        mesh=mesh,
        in_specs=(wide, wide, flat, wide, deep, deep, deep, wide, wide, wide, wide, flat, wide),
        out_specs=(wide, wide),
        check_vma=False,
    )
```

```python
import functools

import jax
import jax.numpy as jnp
from jax import lax
from jax.experimental import pallas as pl
from jax.experimental.pallas import tpu as pltpu
from jax.sharding import PartitionSpec as P

BLOCK = 128
BLK = 128
K = 8
GHOST = 40
ITERS = 3
EXT = BLK + 6 * GHOST
FACE_ROWS = GHOST * 6
RELAXATION = 0.25
TIME_STEP = 1.0 / 60.0
MESH = pl.DeviceIdType.MESH
UNROLL = 4
GROUP = 16
FACE_OF_REGION = (1, 0, 3, 2, 5, 4)


def slot_sums(terms):
    sub = lax.broadcasted_iota(jnp.int32, (8, BLOCK), 0)

    def merge(first, second, bit):
        if second is None:
            return first + pltpu.roll(first, bit, 0)
        low = (sub & bit) == 0
        return jnp.where(low, first, second) + pltpu.roll(jnp.where(low, second, first), bit, 0)

    pairs = [merge(terms[0], terms[1], 1), merge(terms[2], terms[3], 1), merge(terms[4], terms[5], 1)]
    return merge(merge(pairs[0], pairs[1], 2), merge(pairs[2], None, 2), 4)


def kernel(
    vel_h, pos_h, im_h, ii_h, nrm_h, lo_h, lt_h, bias_h, mass_h, pb_h, lane_h, cnt_h, gb_h,
    vout, pout,
    pos, im, ii, nrm, co, ct, base, bias, mass, lane, cnt, inv, imp, vin,
    ext0, ext1, ext2, own, send, tmp, got, pb, gb, rows_of,
    in_sem, send_sem, recv_sem,
):
    gx, gy, gz = lax.axis_index("gx"), lax.axis_index("gy"), lax.axis_index("gz")
    nx, ny, nz = lax.axis_size("gx"), lax.axis_size("gy"), lax.axis_size("gz")
    near = [
        ((gx + nx - 1) % nx, gy, gz), ((gx + 1) % nx, gy, gz),
        (gx, (gy + ny - 1) % ny, gz), (gx, (gy + 1) % ny, gz),
        (gx, gy, (gz + nz - 1) % nz), (gx, gy, (gz + 1) % nz),
    ]
    exts = [ext0, ext1, ext2]

    loads = [
        pltpu.make_async_copy(s, d, in_sem.at[i])
        for i, (s, d) in enumerate([
            (gb_h, gb), (vel_h, vin), (pb_h, pb), (nrm_h, nrm), (lo_h, co), (lt_h, ct), (bias_h, bias),
            (mass_h, mass), (cnt_h, cnt), (im_h, im), (ii_h, ii), (lane_h, lane), (pos_h, pos),
        ])
    ]
    loads[0].start()
    loads[1].start()
    barrier = pltpu.get_barrier_semaphore()
    for device in near:
        pl.semaphore_signal(barrier, inc=1, device_id=device, device_id_type=MESH)
    for load in loads[2:]:
        load.start()

    def column(b):
        return pl.ds(pl.multiple_of(b * BLOCK, BLOCK), BLOCK)

    def loop(count, body, unroll=UNROLL):
        def step(i, carry):
            for u in range(unroll):
                body(i * unroll + u, u)
            return carry
        lax.fori_loop(0, count // unroll, step, 0)

    def copies(round_number):
        made = []
        for region in range(6):
            face = FACE_OF_REGION[region]
            made.append(pltpu.make_async_remote_copy(
                src_ref=send.at[round_number, pl.ds(face * FACE_ROWS, FACE_ROWS)],
                dst_ref=exts[round_number].at[pl.ds((BLK + region * GHOST) * 6, FACE_ROWS)],
                send_sem=send_sem.at[round_number, face],
                recv_sem=recv_sem.at[round_number, face],
                device_id=near[face],
                device_id_type=MESH,
            ))
        return made

    def pack_faces(round_number):
        def body(g, u):
            for face in range(6):
                send[round_number, pl.ds(face * FACE_ROWS + g * 6, 6), :] = own[pl.ds(gb[face, g] * 8, 6), :]
        loop(GHOST, body, 4)

    loads[1].wait()

    def unpack(b, u):
        rows = vin[:, column(b)]
        own[pl.ds(pl.multiple_of(b * 8, 8), 6), :] = rows
        ext0[pl.ds(b * 6, 6), :] = rows
    loop(BLK, unpack)
    loads[0].wait()
    pack_faces(0)
    pl.semaphore_wait(barrier, 6)
    pending = copies(0)
    for copy in pending:
        copy.start()

    for load in loads[2:]:
        load.wait()

    slot_index = lax.broadcasted_iota(jnp.int32, (K, BLOCK), 0)

    def base_of(b, n, c_own, own_rows):
        total = bias[:, column(b)]
        for c in range(3):
            total = total - n[c] * own_rows(c)
            total = total - c_own[c] * own_rows(c + 3)
        base[:, column(b)] = total

    def cross(first, second):
        return [
            first[1] * second[2] - first[2] * second[1],
            first[2] * second[0] - first[0] * second[2],
            first[0] * second[1] - first[1] * second[0],
        ]

    def prepare(b, u):
        cols = column(b)
        n = [nrm[c, :, cols] for c in range(3)]
        c_own = cross([co[c, :, cols] for c in range(3)], n)
        c_other = cross([ct[c, :, cols] for c in range(3)], n)
        for c in range(3):
            co[c, :, cols] = c_own[c]
            ct[c, :, cols] = c_other[c]
        live = slot_index < jnp.broadcast_to(cnt[pl.ds(b, 1), :], (K, BLOCK))
        mass[:, cols] = jnp.where(live, -RELAXATION * mass[:, cols], 0.0)
        row = pl.multiple_of(b * 8, 8)
        inv[pl.ds(row, 3), :] = jnp.broadcast_to(im[pl.ds(b, 1), :], (3, BLOCK))
        inv[pl.ds(row + 3, 3), :] = ii[:, cols]
        base_of(b, n, c_own, lambda c: jnp.broadcast_to(own[pl.ds(row + c, 1), :], (K, BLOCK)))
    loop(BLK, prepare, 2)

    def place(b, u):
        for k in range(K):
            rows_of[b * K + k] = pb[k, b] * 6
    loop(BLK, place, 2)

    for it in range(ITERS):
        ext = exts[it]
        for copy in pending:
            copy.wait()
        last = it == ITERS - 1

        def gather(i):
            rows = rows_of.at[pl.ds(i * (GROUP * K), GROUP * K)]
            for j in range(GROUP * K):
                tmp[pl.ds(j * 9, 8), :] = ext[pl.ds(rows[j], 8), :]

        def span(i):
            return pl.ds(pl.multiple_of(i * (GROUP * BLOCK), GROUP * BLOCK), GROUP * BLOCK)

        def part(u):
            return pl.ds(u * BLOCK, BLOCK)

        def permute(i):
            lane_g = lane.at[:, span(i)]
            for u in range(GROUP):
                lanes = lane_g[:, part(u)]
                for c in range(6):
                    rows = tmp[pl.ds(u * 72 + c, 8, stride=9), :]
                    got[pl.ds((u * 6 + c) * 8, 8), :] = jnp.take_along_axis(rows, lanes, axis=1, mode="promise_in_bounds")

        def update(i):
            wide = span(i)
            base_g, mass_g, imp_g = (r.at[:, wide] for r in (base, mass, imp))
            n_g, own_cross, other_cross = ([r.at[c, :, wide] for c in range(3)] for r in (nrm, co, ct))
            row = pl.multiple_of(i * (GROUP * 8), GROUP * 8)
            own_g, inv_g = own.at[pl.ds(row, GROUP * 8)], inv.at[pl.ds(row, GROUP * 8)]
            if last:
                vout_g, pout_g, pos_g = (r.at[:, wide] for r in (vout, pout, pos))
            else:
                ext_g = exts[it + 1].at[pl.ds(pl.multiple_of(i * (GROUP * 6), GROUP * 6), GROUP * 6)]
            for u in range(GROUP):
                cols = part(u)
                n = [n_g[c][:, cols] for c in range(3)]
                terms = [
                    (n[c] if c < 3 else other_cross[c - 3][:, cols]) * got[pl.ds((u * 6 + c) * 8, 8), :]
                    for c in range(6)
                ]
                total = ((terms[0] + terms[1]) + (terms[2] + terms[3])) + ((terms[4] + terms[5]) + base_g[:, cols])
                step = mass_g[:, cols] * total
                if it == 0:
                    change = jnp.maximum(step, 0.0)
                    new = change
                else:
                    old = imp_g[:, cols]
                    new = jnp.maximum(old + step, 0.0)
                    change = new - old
                if not last:
                    imp_g[:, cols] = new
                sums = slot_sums([change * (n[c] if c < 3 else own_cross[c - 3][:, cols]) for c in range(6)])
                moved = (own_g[pl.ds(u * 8, 8), :] - inv_g[pl.ds(u * 8, 8), :] * sums)[:6]
                if last:
                    vout_g[:, cols] = moved
                    pout_g[:, cols] = pos_g[:, cols] + TIME_STEP * moved[:3]
                else:
                    own_g[pl.ds(u * 8, 6), :] = moved
                    ext_g[pl.ds(u * 6, 6), :] = moved

        groups = BLK // GROUP
        gather(0)
        permute(0)
        gather(1)

        def stages(i, carry):
            update(i)
            permute(jnp.minimum(i + 1, groups - 1))
            gather(jnp.minimum(i + 2, groups - 1))
            return carry
        lax.fori_loop(0, groups, stages, 0)

        if not last:
            pack_faces(it + 1)
            pending = copies(it + 1)
            for copy in pending:
                copy.start()

            def rebase(b, u):
                cols = column(b)
                row = pl.multiple_of(b * 8, 8)
                base_of(
                    b, [nrm[c, :, cols] for c in range(3)], [co[c, :, cols] for c in range(3)],
                    lambda c: jnp.broadcast_to(own[pl.ds(row + c, 1), :], (K, BLOCK)),
                )
            loop(BLK, rebase)


def per_device(
    velocity, positions, inverse_mass, inverse_inertia, normals, lever_own, lever_other, speed_bias, contact_mass,
    partner_block, partner_lane, slot_counts, ghost_blocks,
):
    bodies = BLK * BLOCK
    slots = pltpu.VMEM((K, bodies), jnp.float32)
    vectors = pltpu.VMEM((3, K, bodies), jnp.float32)
    table = pltpu.VMEM((EXT * 6 + 8, BLOCK), jnp.float32)
    hbm = pl.BlockSpec(memory_space=pl.ANY)
    vmem = pl.BlockSpec(memory_space=pltpu.VMEM)
    return pl.pallas_call(
        kernel,
        out_shape=(
            jax.ShapeDtypeStruct((6, bodies), jnp.float32),
            jax.ShapeDtypeStruct((3, bodies), jnp.float32),
        ),
        in_specs=[hbm] * 13,
        out_specs=(vmem, vmem),
        scratch_shapes=[
            pltpu.VMEM((3, bodies), jnp.float32),
            pltpu.VMEM((BLK, BLOCK), jnp.float32),
            pltpu.VMEM((3, bodies), jnp.float32),
            vectors, vectors, vectors,
            slots, slots, slots,
            pltpu.VMEM((K, bodies), jnp.int32),
            pltpu.VMEM((BLK, BLOCK), jnp.int32),
            pltpu.VMEM((BLK * 8, BLOCK), jnp.float32),
            slots,
            pltpu.VMEM((6, bodies), jnp.float32),
            table, table, table,
            pltpu.VMEM((BLK * 8, BLOCK), jnp.float32),
            pltpu.VMEM((ITERS, 6 * FACE_ROWS, BLOCK), jnp.float32),
            pltpu.VMEM((GROUP * 72 + 16, BLOCK), jnp.float32),
            pltpu.VMEM((GROUP * 48, BLOCK), jnp.float32),
            pltpu.SMEM((K, BLK), jnp.int32),
            pltpu.SMEM((6, GHOST), jnp.int32),
            pltpu.SMEM((BLK * K,), jnp.int32),
            pltpu.SemaphoreType.DMA((13,)),
            pltpu.SemaphoreType.DMA((ITERS, 6)),
            pltpu.SemaphoreType.DMA((ITERS, 6)),
        ],
        compiler_params=pltpu.CompilerParams(collective_id=0, has_side_effects=True),
    )(
        velocity, positions, inverse_mass.reshape(BLK, BLOCK), inverse_inertia, normals, lever_own, lever_other,
        speed_bias, contact_mass, partner_block, partner_lane, slot_counts.reshape(BLK, BLOCK), ghost_blocks,
    )


def solution(mesh):
    every = ("gx", "gy", "gz")
    flat, wide, deep = P(every), P(None, every), P(None, None, every)
    return jax.shard_map(
        per_device,
        mesh=mesh,
        in_specs=(wide, wide, flat, wide, deep, deep, deep, wide, wide, wide, wide, flat, wide),
        out_specs=(wide, wide),
        check_vma=False,
    )
```

```python
import functools

import jax
import jax.numpy as jnp
from jax import lax
from jax.experimental import pallas as pl
from jax.experimental.pallas import tpu as pltpu
from jax.sharding import PartitionSpec as P

BLOCK = 128
BLK = 128
K = 8
GHOST = 40
ITERS = 3
EXT = BLK + 6 * GHOST
FACE_ROWS = GHOST * 6
RELAXATION = 0.25
TIME_STEP = 1.0 / 60.0
MESH = pl.DeviceIdType.MESH
UNROLL = 4
GROUP = 16
FACE_OF_REGION = (1, 0, 3, 2, 5, 4)


def slot_sums(terms):
    sub = lax.broadcasted_iota(jnp.int32, (8, BLOCK), 0)

    def merge(first, second, bit):
        if second is None:
            return first + pltpu.roll(first, bit, 0)
        low = (sub & bit) == 0
        return jnp.where(low, first, second) + pltpu.roll(jnp.where(low, second, first), bit, 0)

    pairs = [merge(terms[0], terms[1], 1), merge(terms[2], terms[3], 1), merge(terms[4], terms[5], 1)]
    return merge(merge(pairs[0], pairs[1], 2), merge(pairs[2], None, 2), 4)


def kernel(
    vel_h, pos_h, im_h, ii_h, nrm_h, lo_h, lt_h, bias_h, mass_h, pb_h, lane_h, cnt_h, gb_h,
    vout, pout,
    pos, im, ii, nrm, co, ct, base, bias, mass, lane, cnt, inv, imp, vin,
    ext0, ext1, ext2, own, send, tmp, got, pb, gb, rows_of,
    in_sem, send_sem, recv_sem,
):
    gx, gy, gz = lax.axis_index("gx"), lax.axis_index("gy"), lax.axis_index("gz")
    nx, ny, nz = lax.axis_size("gx"), lax.axis_size("gy"), lax.axis_size("gz")
    near = [
        ((gx + nx - 1) % nx, gy, gz), ((gx + 1) % nx, gy, gz),
        (gx, (gy + ny - 1) % ny, gz), (gx, (gy + 1) % ny, gz),
        (gx, gy, (gz + nz - 1) % nz), (gx, gy, (gz + 1) % nz),
    ]
    exts = [ext0, ext1, ext2]

    loads = [
        pltpu.make_async_copy(s, d, in_sem.at[i])
        for i, (s, d) in enumerate([
            (gb_h, gb), (vel_h, vin), (pb_h, pb), (nrm_h, nrm), (lo_h, co), (lt_h, ct), (bias_h, bias),
            (mass_h, mass), (cnt_h, cnt), (im_h, im), (ii_h, ii), (lane_h, lane), (pos_h, pos),
        ])
    ]
    loads[0].start()
    loads[1].start()
    barrier = pltpu.get_barrier_semaphore()
    for device in near:
        pl.semaphore_signal(barrier, inc=1, device_id=device, device_id_type=MESH)
    for load in loads[2:]:
        load.start()

    def column(b):
        return pl.ds(pl.multiple_of(b * BLOCK, BLOCK), BLOCK)

    def loop(count, body, unroll=UNROLL):
        def step(i, carry):
            for u in range(unroll):
                body(i * unroll + u, u)
            return carry
        lax.fori_loop(0, count // unroll, step, 0)

    def copies(round_number):
        made = []
        for region in range(6):
            face = FACE_OF_REGION[region]
            made.append(pltpu.make_async_remote_copy(
                src_ref=send.at[round_number, pl.ds(face * FACE_ROWS, FACE_ROWS)],
                dst_ref=exts[round_number].at[pl.ds((BLK + region * GHOST) * 6, FACE_ROWS)],
                send_sem=send_sem.at[round_number, face],
                recv_sem=recv_sem.at[round_number, face],
                device_id=near[face],
                device_id_type=MESH,
            ))
        return made

    def pack_faces(round_number):
        def body(g, u):
            for face in range(6):
                send[round_number, pl.ds(face * FACE_ROWS + g * 6, 6), :] = own[pl.ds(gb[face, g] * 8, 6), :]
        loop(GHOST, body, 4)

    loads[1].wait()

    def unpack(b, u):
        rows = vin[:, column(b)]
        own[pl.ds(pl.multiple_of(b * 8, 8), 6), :] = rows
        ext0[pl.ds(b * 6, 6), :] = rows
    loop(BLK, unpack)
    loads[0].wait()
    pack_faces(0)
    pl.semaphore_wait(barrier, 6)
    pending = copies(0)
    for copy in pending:
        copy.start()

    for load in loads[2:]:
        load.wait()

    slot_index = lax.broadcasted_iota(jnp.int32, (K, BLOCK), 0)

    def base_of(b, n, c_own, own_rows):
        total = bias[:, column(b)]
        for c in range(3):
            total = total - n[c] * own_rows(c)
            total = total - c_own[c] * own_rows(c + 3)
        base[:, column(b)] = total

    def cross(first, second):
        return [
            first[1] * second[2] - first[2] * second[1],
            first[2] * second[0] - first[0] * second[2],
            first[0] * second[1] - first[1] * second[0],
        ]

    def prepare(b, u):
        cols = column(b)
        n = [nrm[c, :, cols] for c in range(3)]
        c_own = cross([co[c, :, cols] for c in range(3)], n)
        c_other = cross([ct[c, :, cols] for c in range(3)], n)
        for c in range(3):
            co[c, :, cols] = c_own[c]
            ct[c, :, cols] = c_other[c]
        live = slot_index < jnp.broadcast_to(cnt[pl.ds(b, 1), :], (K, BLOCK))
        mass[:, cols] = jnp.where(live, -RELAXATION * mass[:, cols], 0.0)
        row = pl.multiple_of(b * 8, 8)
        inv[pl.ds(row, 3), :] = jnp.broadcast_to(im[pl.ds(b, 1), :], (3, BLOCK))
        inv[pl.ds(row + 3, 3), :] = ii[:, cols]
        base_of(b, n, c_own, lambda c: jnp.broadcast_to(own[pl.ds(row + c, 1), :], (K, BLOCK)))
    loop(BLK, prepare, 2)

    def place(b, u):
        for k in range(K):
            rows_of[b * K + k] = pb[k, b] * 6
    loop(BLK, place, 2)

    for it in range(ITERS):
        ext = exts[it]
        for copy in pending:
            copy.wait()
        last = it == ITERS - 1

        def gather(i):
            rows = rows_of.at[pl.ds(i * (GROUP * K), GROUP * K)]
            for j in range(GROUP * K):
                tmp[pl.ds(j * 9, 8), :] = ext[pl.ds(rows[j], 8), :]

        def span(i):
            return pl.ds(pl.multiple_of(i * (GROUP * BLOCK), GROUP * BLOCK), GROUP * BLOCK)

        def part(u):
            return pl.ds(u * BLOCK, BLOCK)

        def permute(i):
            lane_g = lane.at[:, span(i)]
            for u in range(GROUP):
                lanes = lane_g[:, part(u)]
                for c in range(6):
                    rows = tmp[pl.ds(u * 72 + c, 8, stride=9), :]
                    got[pl.ds((u * 6 + c) * 8, 8), :] = jnp.take_along_axis(rows, lanes, axis=1, mode="promise_in_bounds")

        def update(i):
            wide = span(i)
            base_g, mass_g, imp_g = (r.at[:, wide] for r in (base, mass, imp))
            n_g, own_cross, other_cross = ([r.at[c, :, wide] for c in range(3)] for r in (nrm, co, ct))
            row = pl.multiple_of(i * (GROUP * 8), GROUP * 8)
            own_g, inv_g = own.at[pl.ds(row, GROUP * 8)], inv.at[pl.ds(row, GROUP * 8)]
            if last:
                vout_g, pout_g, pos_g = (r.at[:, wide] for r in (vout, pout, pos))
            else:
                ext_g = exts[it + 1].at[pl.ds(pl.multiple_of(i * (GROUP * 6), GROUP * 6), GROUP * 6)]
            for u in range(GROUP):
                cols = part(u)
                n = [n_g[c][:, cols] for c in range(3)]
                terms = [
                    (n[c] if c < 3 else other_cross[c - 3][:, cols]) * got[pl.ds((u * 6 + c) * 8, 8), :]
                    for c in range(6)
                ]
                total = ((terms[0] + terms[1]) + (terms[2] + terms[3])) + ((terms[4] + terms[5]) + base_g[:, cols])
                step = mass_g[:, cols] * total
                if it == 0:
                    change = jnp.maximum(step, 0.0)
                    new = change
                else:
                    old = imp_g[:, cols]
                    new = jnp.maximum(old + step, 0.0)
                    change = new - old
                if not last:
                    imp_g[:, cols] = new
                sums = slot_sums([change * (n[c] if c < 3 else own_cross[c - 3][:, cols]) for c in range(6)])
                moved = (own_g[pl.ds(u * 8, 8), :] - inv_g[pl.ds(u * 8, 8), :] * sums)[:6]
                if last:
                    vout_g[:, cols] = moved
                    pout_g[:, cols] = pos_g[:, cols] + TIME_STEP * moved[:3]
                else:
                    own_g[pl.ds(u * 8, 6), :] = moved
                    ext_g[pl.ds(u * 6, 6), :] = moved

        groups = BLK // GROUP
        gather(0)
        permute(0)
        gather(1)

        def stages(i, carry):
            update(i)
            permute(jnp.minimum(i + 1, groups - 1))
            gather(jnp.minimum(i + 2, groups - 1))
            return carry
        lax.fori_loop(0, groups, stages, 0)

        if not last:
            pack_faces(it + 1)
            pending = copies(it + 1)
            for copy in pending:
                copy.start()

            def rebase(b, u):
                cols = column(b)
                row = pl.multiple_of(b * 8, 8)
                base_of(
                    b, [nrm[c, :, cols] for c in range(3)], [co[c, :, cols] for c in range(3)],
                    lambda c: jnp.broadcast_to(own[pl.ds(row + c, 1), :], (K, BLOCK)),
                )
            loop(BLK, rebase)


def finish(moved, placed, vel_out, pos_out, sems):
    writes = [pltpu.make_async_copy(moved, vel_out, sems.at[0]), pltpu.make_async_copy(placed, pos_out, sems.at[1])]
    for write in writes:
        write.start()
    for write in writes:
        write.wait()


def per_device(
    velocity, positions, inverse_mass, inverse_inertia, normals, lever_own, lever_other, speed_bias, contact_mass,
    partner_block, partner_lane, slot_counts, ghost_blocks,
):
    bodies = BLK * BLOCK
    slots = pltpu.VMEM((K, bodies), jnp.float32)
    vectors = pltpu.VMEM((3, K, bodies), jnp.float32)
    table = pltpu.VMEM((EXT * 6 + 8, BLOCK), jnp.float32)
    hbm = pl.BlockSpec(memory_space=pl.ANY)
    vmem = pl.BlockSpec(memory_space=pltpu.VMEM)
    moved, placed = pl.pallas_call(
        kernel,
        out_shape=(pltpu.VMEM((6, bodies), jnp.float32), pltpu.VMEM((3, bodies), jnp.float32)),
        in_specs=[hbm] * 13,
        out_specs=(vmem, vmem),
        scratch_shapes=[
            pltpu.VMEM((3, bodies), jnp.float32),
            pltpu.VMEM((BLK, BLOCK), jnp.float32),
            pltpu.VMEM((3, bodies), jnp.float32),
            vectors, vectors, vectors,
            slots, slots, slots,
            pltpu.VMEM((K, bodies), jnp.int32),
            pltpu.VMEM((BLK, BLOCK), jnp.int32),
            pltpu.VMEM((BLK * 8, BLOCK), jnp.float32),
            slots,
            pltpu.VMEM((6, bodies), jnp.float32),
            table, table, table,
            pltpu.VMEM((BLK * 8, BLOCK), jnp.float32),
            pltpu.VMEM((ITERS, 6 * FACE_ROWS, BLOCK), jnp.float32),
            pltpu.VMEM((GROUP * 72 + 16, BLOCK), jnp.float32),
            pltpu.VMEM((GROUP * 48, BLOCK), jnp.float32),
            pltpu.SMEM((K, BLK), jnp.int32),
            pltpu.SMEM((6, GHOST), jnp.int32),
            pltpu.SMEM((BLK * K,), jnp.int32),
            pltpu.SemaphoreType.DMA((13,)),
            pltpu.SemaphoreType.DMA((ITERS, 6)),
            pltpu.SemaphoreType.DMA((ITERS, 6)),
        ],
        compiler_params=pltpu.CompilerParams(collective_id=0, has_side_effects=True),
    )(
        velocity, positions, inverse_mass.reshape(BLK, BLOCK), inverse_inertia, normals, lever_own, lever_other,
        speed_bias, contact_mass, partner_block, partner_lane, slot_counts.reshape(BLK, BLOCK), ghost_blocks,
    )
    return pl.pallas_call(
        finish,
        out_shape=(
            jax.ShapeDtypeStruct((6, bodies), jnp.float32),
            jax.ShapeDtypeStruct((3, bodies), jnp.float32),
        ),
        in_specs=[vmem, vmem],
        out_specs=(hbm, hbm),
        scratch_shapes=[pltpu.SemaphoreType.DMA((2,))],
    )(pltpu.with_memory_space_constraint(moved, pltpu.VMEM), pltpu.with_memory_space_constraint(placed, pltpu.VMEM))


def solution(mesh):
    every = ("gx", "gy", "gz")
    flat, wide, deep = P(every), P(None, every), P(None, None, every)
    return jax.shard_map(
        per_device,
        mesh=mesh,
        in_specs=(wide, wide, flat, wide, deep, deep, deep, wide, wide, wide, wide, flat, wide),
        out_specs=(wide, wide),
        check_vma=False,
    )
```

```python
import functools

import jax
import jax.numpy as jnp
from jax import lax
from jax.experimental import pallas as pl
from jax.experimental.pallas import tpu as pltpu
from jax.sharding import PartitionSpec as P

BLOCK = 128
BLK = 128
K = 8
GHOST = 40
ITERS = 3
EXT = BLK + 6 * GHOST
FACE_ROWS = GHOST * 6
RELAXATION = 0.25
TIME_STEP = 1.0 / 60.0
MESH = pl.DeviceIdType.MESH
UNROLL = 4
GROUP = 16
SEND_ROW, BLOCK_AT, PLACE_OF = 8, 16, 24
NORMAL, OWN_CROSS, OTHER_CROSS, BASE, BIAS, MASS, IMPULSE, PLANES = 0, 3, 6, 9, 10, 11, 12, 13
ROW = 4


def slot_sums(terms):
    sub = lax.broadcasted_iota(jnp.int32, (8, BLOCK), 0)

    def merge(first, second, bit):
        if second is None:
            return first + pltpu.roll(first, bit, 0)
        low = (sub & bit) == 0
        return jnp.where(low, first, second) + pltpu.roll(jnp.where(low, second, first), bit, 0)

    pairs = [merge(terms[0], terms[1], 1), merge(terms[2], terms[3], 1), merge(terms[4], terms[5], 1)]
    return merge(merge(pairs[0], pairs[1], 2), merge(pairs[2], None, 2), 4)


def pick_lanes(rows, lanes):
    numbers = lax.GatherDimensionNumbers(
        offset_dims=(), collapsed_slice_dims=(1,), start_index_map=(1,),
        operand_batching_dims=(0,), start_indices_batching_dims=(0,),
    )
    return lax.gather(rows, lanes[:, :, None], numbers, (1, 1), mode=lax.GatherScatterMode.PROMISE_IN_BOUNDS)


def kernel(
    vel_h, pos_h, im_h, ii_h, nrm_h, lo_h, lt_h, bias_h, mass_h, pb_h, lane_h, cnt_h, gb_h,
    vout, pout,
    pos, im, ii, raw, slots, raw_lane, lane, cnt, bodies, vin,
    ext0, ext1, ext2, send, tmp, got, pb, gb, entries, ranks, tables, block_of, send_rows, place_row, rows_of,
    in_sem, send_sem, recv_sem,
):
    gx, gy, gz = lax.axis_index("gx"), lax.axis_index("gy"), lax.axis_index("gz")
    nx, ny, nz = lax.axis_size("gx"), lax.axis_size("gy"), lax.axis_size("gz")
    near = [
        ((gx + nx - 1) % nx, gy, gz), ((gx + 1) % nx, gy, gz),
        (gx, (gy + ny - 1) % ny, gz), (gx, (gy + 1) % ny, gz),
        (gx, gy, (gz + nz - 1) % nz), (gx, gy, (gz + 1) % nz),
    ]
    exts = [ext0, ext1, ext2]
    own, inv = bodies.at[0], bodies.at[1]
    nrm, co, ct = (slots.at[pl.ds(first, 3)] for first in (NORMAL, OWN_CROSS, OTHER_CROSS))
    base, bias, mass = (slots.at[which] for which in (BASE, BIAS, MASS))

    loads = [
        pltpu.make_async_copy(s, d, in_sem.at[i])
        for i, (s, d) in enumerate([
            (gb_h, gb), (vel_h, vin), (pb_h, pb), (nrm_h, raw.at[pl.ds(0, 3)]), (lo_h, raw.at[pl.ds(3, 3)]), (lt_h, raw.at[pl.ds(6, 3)]), (bias_h, raw.at[9]),
            (mass_h, raw.at[10]), (cnt_h, cnt), (im_h, im), (ii_h, ii), (lane_h, raw_lane), (pos_h, pos),
        ])
    ]
    for load in loads[:3]:
        load.start()
    barrier = pltpu.get_barrier_semaphore()
    for device in near:
        pl.semaphore_signal(barrier, inc=1, device_id=device, device_id_type=MESH)
    for load in loads[3:]:
        load.start()

    def column(b):
        return pl.ds(pl.multiple_of(b * BLOCK, BLOCK), BLOCK)

    def loop(count, body, unroll=UNROLL):
        def step(i, carry):
            for u in range(unroll):
                body(i * unroll + u, u)
            return carry
        lax.fori_loop(0, count // unroll, step, 0)

    far_x = gx % 2
    far_y = jnp.where(gy % ROW == 0, 2, 3)
    far_x_near = (jnp.where(far_x == 0, near[0][0], near[1][0]), gy, gz)
    pair_near = (jnp.where(far_x == 0, near[1][0], near[0][0]), gy, gz)
    far_y_near = (gx, jnp.where(far_y == 2, near[2][1], near[3][1]), gz)
    short_y_near = (gx, jnp.where(far_y == 2, near[3][1], near[2][1]), gz)
    first_face = [(far_x, far_x_near)]
    second_face = [(far_y, far_y_near)]
    other_faces = [(4, near[4]), (5, near[5]), (5 - far_y, short_y_near), (1 - far_x, pair_near)]

    def face_copy(round_number, face, device):
        region = face + 1 - 2 * (face % 2)
        return pltpu.make_async_remote_copy(
            src_ref=send.at[round_number, pl.ds(face * FACE_ROWS, FACE_ROWS)],
            dst_ref=exts[round_number].at[pl.ds((BLK + region * GHOST) * 6, FACE_ROWS)],
            send_sem=send_sem.at[round_number, face],
            recv_sem=recv_sem.at[round_number, face],
            device_id=device,
            device_id_type=MESH,
        )

    def receive(round_number):
        for face in range(6):
            face_copy(round_number, face, near[face]).wait()

    def send_faces(round_number, faces):
        def body(g, u):
            for face, _ in faces:
                row = send_rows[face * GHOST + g]
                send[round_number, pl.ds(face * FACE_ROWS + g * 6, 6), :] = own[pl.ds(row, 6), :]
        loop(GHOST, body, 4)
        for face, device in faces:
            face_copy(round_number, face, device).start()

    loads[0].wait()
    loads[2].wait()
    down = lax.broadcasted_iota(jnp.int32, (BLK, BLK), 0)
    across = lax.broadcasted_iota(jnp.int32, (BLK, BLK), 1)
    sublane = lax.broadcasted_iota(jnp.int32, (8, BLK), 0)
    number = lax.broadcasted_iota(jnp.int32, (8, BLK), 1)
    found = jnp.zeros((8, BLK), jnp.int32)
    for face in range(6):
        row = jnp.zeros((8, BLK), jnp.int32)
        for g in range(GHOST):
            row = jnp.where(number == g, gb[face, g], row)
        found = jnp.where(sublane == face, row, found)
    entries[...] = found

    def in_face(face):
        found = jnp.broadcast_to(entries[pl.ds(face, 1), :], (BLK, BLK)) == down
        return jnp.sum(jnp.where(found & (across < GHOST), 1, 0), axis=1, keepdims=True) > 0

    def to_row(column):
        return jnp.sum(jnp.where(down == across, column, 0), axis=0, keepdims=True)

    def to_column(row):
        return jnp.sum(jnp.where(down == across, row, 0), axis=1, keepdims=True)

    key = jnp.where(in_face(far_x), 0, jnp.where(in_face(far_y), BLK, 2 * BLK)) + down[:, :1]
    place_of = jnp.sum(jnp.where(key < to_row(key), 1, 0), axis=0, keepdims=True)
    block_at = jnp.sum(jnp.where(to_column(place_of) == across, down, 0), axis=0, keepdims=True)
    place_of, block_at = (jnp.broadcast_to(jnp.clip(row, 0, BLK - 1), (8, BLK)) for row in (place_of, block_at))
    partner = pick_lanes(pb[...], block_at)
    partner_place = pick_lanes(place_of, jnp.minimum(partner, BLK - 1))
    ranks[pl.ds(0, 8), :] = 6 * jnp.where(partner < BLK, partner_place, partner)
    ranks[pl.ds(SEND_ROW, 8), :] = 8 * pick_lanes(place_of, entries[...])
    ranks[pl.ds(BLOCK_AT, 8), :] = block_at
    ranks[pl.ds(PLACE_OF, 8), :] = place_of
    to_scalars = pltpu.make_async_copy(ranks, tables, in_sem.at[0])
    to_scalars.start()
    to_scalars.wait()

    def bounded(value, most):
        return jnp.minimum(jnp.maximum(value, 0), most)

    def orders(b, u):
        block_of[b] = bounded(tables[BLOCK_AT, b], BLK - 1)
    loop(BLK, orders)

    def entry_rows(g, u):
        for face in range(6):
            send_rows[face * GHOST + g] = bounded(tables[SEND_ROW + face, g], (BLK - 1) * 8)
    loop(GHOST, entry_rows)

    loads[1].wait()

    def unpack(i, u):
        rows = vin[:, pl.ds(block_of[i] * BLOCK, BLOCK)]
        own[pl.ds(pl.multiple_of(i * 8, 8), 6), :] = rows
        ext0[pl.ds(i * 6, 6), :] = rows
    loop(BLK, unpack)

    pl.semaphore_wait(barrier, 6)
    for faces in (first_face, second_face, other_faces):
        send_faces(0, faces)

    for load in loads[3:]:
        load.wait()

    slot_index = lax.broadcasted_iota(jnp.int32, (K, BLOCK), 0)

    def base_of(b, n, c_own, own_rows, total):
        for c in range(3):
            total = total - n[c] * own_rows(c)
            total = total - c_own[c] * own_rows(c + 3)
        base[:, column(b)] = total

    def cross(first, second):
        return [
            first[1] * second[2] - first[2] * second[1],
            first[2] * second[0] - first[0] * second[2],
            first[0] * second[1] - first[1] * second[0],
        ]

    def prepare(i, u):
        b = block_of[i]
        cols = column(i)
        source = [raw[c, :, pl.ds(b * BLOCK, BLOCK)] for c in range(11)]
        n = source[:3]
        c_own = cross([source[3 + c] for c in range(3)], n)
        c_other = cross([source[6 + c] for c in range(3)], n)
        target = slots.at[:, :, cols]
        for c in range(3):
            target[NORMAL + c] = n[c]
            target[OWN_CROSS + c] = c_own[c]
            target[OTHER_CROSS + c] = c_other[c]
        lane[:, cols] = raw_lane[:, pl.ds(b * BLOCK, BLOCK)]
        live = slot_index < jnp.broadcast_to(cnt[pl.ds(b, 1), :], (K, BLOCK))
        target[MASS] = jnp.where(live, -RELAXATION * source[10], 0.0)
        target[BIAS] = source[9]
        row = pl.multiple_of(i * 8, 8)
        inv[pl.ds(row, 3), :] = jnp.broadcast_to(im[pl.ds(b, 1), :], (3, BLOCK))
        inv[pl.ds(row + 3, 3), :] = ii[:, pl.ds(b * BLOCK, BLOCK)]
        base_of(i, n, c_own, lambda c: jnp.broadcast_to(own[pl.ds(row + c, 1), :], (K, BLOCK)), source[9])
    loop(BLK, prepare, 2)

    def scalars(i, u):
        place_row[i] = bounded(tables[PLACE_OF, i], BLK - 1) * 8
        for k in range(K):
            rows_of[i * K + k] = bounded(tables[k, i], (EXT - 1) * 6)
    loop(BLK, scalars, 2)

    for it in range(ITERS):
        ext = exts[it]
        receive(it)
        last = it == ITERS - 1

        def gather(rows_at):
            for u, rows in enumerate(rows_at):
                for k in range(K):
                    tmp[pl.ds((u * K + k) * 9, 8), :] = ext[pl.ds(rows[k], 8), :]

        def permute(lanes_of):
            for u, lanes in enumerate(lanes_of):
                for c in range(6):
                    rows = tmp[pl.ds(u * 72 + c, 8, stride=9), :]
                    got[pl.ds((u * 6 + c) * 8, 8), :] = pick_lanes(rows, lanes)

        def impulse_and_moved(u, plane, own_b, inv_b):
            normal = [plane(NORMAL + c) for c in range(3)]
            terms = [(normal[c] if c < 3 else plane(OTHER_CROSS + c - 3)) * got[pl.ds((u * 6 + c) * 8, 8), :] for c in range(6)]
            total = ((terms[0] + terms[1]) + (terms[2] + terms[3])) + ((terms[4] + terms[5]) + plane(BASE))
            step = plane(MASS) * total
            if it == 0:
                new = jnp.maximum(step, 0.0)
                change = new
            else:
                old = plane(IMPULSE)
                new = jnp.maximum(old + step, 0.0)
                change = new - old
            sums = slot_sums([change * (normal[c] if c < 3 else plane(OWN_CROSS + c - 3)) for c in range(6)])
            return new, (own_b - inv_b * sums)[:6]

        def wide(i):
            return pl.ds(pl.multiple_of(i * (GROUP * BLOCK), GROUP * BLOCK), GROUP * BLOCK)

        def rows_at(i):
            rows = rows_of.at[pl.ds(i * (GROUP * K), GROUP * K)]
            return [[rows[u * K + k] for k in range(K)] for u in range(GROUP)]

        def lanes_at(i):
            lane_g = lane.at[:, wide(i)]
            return [lane_g[:, pl.ds(u * BLOCK, BLOCK)] for u in range(GROUP)]

        def update(i):
            slots_g = slots.at[:, :, wide(i)]
            bodies_g = bodies.at[:, pl.ds(pl.multiple_of(i * (GROUP * 8), GROUP * 8), GROUP * 8)]
            if not last:
                ext_g = exts[it + 1].at[pl.ds(pl.multiple_of(i * (GROUP * 6), GROUP * 6), GROUP * 6)]
            for u in range(GROUP):
                cols, row = pl.ds(u * BLOCK, BLOCK), pl.ds(u * 8, 8)
                new, moved = impulse_and_moved(u, lambda p: slots_g[p, :, cols], bodies_g[0, row, :], bodies_g[1, row, :])
                bodies_g[0, pl.ds(u * 8, 6), :] = moved
                if not last:
                    slots_g[IMPULSE, :, cols] = new
                    ext_g[pl.ds(u * 6, 6), :] = moved

        groups = BLK // GROUP

        def stages(i, carry):
            update(i)
            permute(lanes_at(jnp.minimum(i + 1, groups - 1)))
            gather(rows_at(jnp.minimum(i + 2, groups - 1)))
            return carry

        gather(rows_at(0))
        permute(lanes_at(0))
        gather(rows_at(1))
        if last:
            lax.fori_loop(0, groups, stages, 0)

            def finished(b, u):
                cols = column(b)
                moved = own[pl.ds(place_row[b], 6), :]
                vout[:, cols] = moved
                pout[:, cols] = pos[:, cols] + TIME_STEP * moved[:3]
            loop(BLK, finished)
        else:
            done = 0
            for blocks, faces in ((GHOST, first_face), (2 * GHOST, second_face), (BLK, other_faces)):
                until = -(-blocks // GROUP)
                lax.fori_loop(done, until, stages, 0)
                send_faces(it + 1, faces)
                done = until

            def rebase(b, u):
                cols = column(b)
                row = pl.multiple_of(b * 8, 8)
                base_of(
                    b, [nrm[c, :, cols] for c in range(3)], [co[c, :, cols] for c in range(3)],
                    lambda c: jnp.broadcast_to(own[pl.ds(row + c, 1), :], (K, BLOCK)), bias[:, cols],
                )
            loop(BLK, rebase)


def finish(moved, placed, vel_out, pos_out, sems):
    writes = [pltpu.make_async_copy(moved, vel_out, sems.at[0]), pltpu.make_async_copy(placed, pos_out, sems.at[1])]
    for write in writes:
        write.start()
    for write in writes:
        write.wait()


def per_device(
    velocity, positions, inverse_mass, inverse_inertia, normals, lever_own, lever_other, speed_bias, contact_mass,
    partner_block, partner_lane, slot_counts, ghost_blocks,
):
    bodies = BLK * BLOCK
    table = pltpu.VMEM((EXT * 6 + 8, BLOCK), jnp.float32)
    hbm = pl.BlockSpec(memory_space=pl.ANY)
    vmem = pl.BlockSpec(memory_space=pltpu.VMEM)
    moved, placed = pl.pallas_call(
        kernel,
        out_shape=(pltpu.VMEM((6, bodies), jnp.float32), pltpu.VMEM((3, bodies), jnp.float32)),
        in_specs=[hbm] * 13,
        out_specs=(vmem, vmem),
        scratch_shapes=[
            pltpu.VMEM((3, bodies), jnp.float32),
            pltpu.VMEM((BLK, BLOCK), jnp.float32),
            pltpu.VMEM((3, bodies), jnp.float32),
            pltpu.VMEM((11, K, bodies), jnp.float32),
            pltpu.VMEM((PLANES, K, bodies), jnp.float32),
            pltpu.VMEM((K, bodies), jnp.int32),
            pltpu.VMEM((K, bodies), jnp.int32),
            pltpu.VMEM((BLK, BLOCK), jnp.int32),
            pltpu.VMEM((2, BLK * 8, BLOCK), jnp.float32),
            pltpu.VMEM((6, bodies), jnp.float32),
            table, table, table,
            pltpu.VMEM((ITERS, 6 * FACE_ROWS, BLOCK), jnp.float32),
            pltpu.VMEM((GROUP * 72 + 16, BLOCK), jnp.float32),
            pltpu.VMEM((GROUP * 48, BLOCK), jnp.float32),
            pltpu.VMEM((K, BLK), jnp.int32),
            pltpu.SMEM((6, GHOST), jnp.int32),
            pltpu.VMEM((8, BLK), jnp.int32),
            pltpu.VMEM((32, BLK), jnp.int32),
            pltpu.SMEM((32, BLK), jnp.int32),
            pltpu.SMEM((BLK,), jnp.int32),
            pltpu.SMEM((6 * GHOST,), jnp.int32),
            pltpu.SMEM((BLK,), jnp.int32),
            pltpu.SMEM((BLK * K,), jnp.int32),
            pltpu.SemaphoreType.DMA((13,)),
            pltpu.SemaphoreType.DMA((ITERS, 6)),
            pltpu.SemaphoreType.DMA((ITERS, 6)),
        ],
        compiler_params=pltpu.CompilerParams(collective_id=0, has_side_effects=True),
    )(
        velocity, positions, inverse_mass.reshape(BLK, BLOCK), inverse_inertia, normals, lever_own, lever_other,
        speed_bias, contact_mass, partner_block, partner_lane, slot_counts.reshape(BLK, BLOCK), ghost_blocks,
    )
    return pl.pallas_call(
        finish,
        out_shape=(
            jax.ShapeDtypeStruct((6, bodies), jnp.float32),
            jax.ShapeDtypeStruct((3, bodies), jnp.float32),
        ),
        in_specs=[vmem, vmem],
        out_specs=(hbm, hbm),
        scratch_shapes=[pltpu.SemaphoreType.DMA((2,))],
    )(pltpu.with_memory_space_constraint(moved, pltpu.VMEM), pltpu.with_memory_space_constraint(placed, pltpu.VMEM))


def solution(mesh):
    every = ("gx", "gy", "gz")
    flat, wide, deep = P(every), P(None, every), P(None, None, every)
    return jax.shard_map(
        per_device,
        mesh=mesh,
        in_specs=(wide, wide, flat, wide, deep, deep, deep, wide, wide, wide, wide, flat, wide),
        out_specs=(wide, wide),
        check_vma=False,
    )
```

```python
import functools

import jax
import jax.numpy as jnp
from jax import lax
from jax.experimental import pallas as pl
from jax.experimental.pallas import tpu as pltpu
from jax.sharding import PartitionSpec as P

BLOCK = 128
BLK = 128
K = 8
GHOST = 40
ITERS = 3
EXT = BLK + 6 * GHOST
FACE_ROWS = GHOST * 6
TABLE_ROWS = 4096
RELAXATION = 0.25
TIME_STEP = 1.0 / 60.0
MESH = pl.DeviceIdType.MESH
UNROLL = 4
GROUP = 16
SEND_ROW, BLOCK_AT, PLACE_OF = 8, 16, 24
NORMAL, OWN_CROSS, OTHER_CROSS, BASE, BIAS, MASS, IMPULSE, PLANES = 0, 3, 6, 9, 10, 11, 12, 13
ROW = 4


def slot_sums(terms):
    sub = lax.broadcasted_iota(jnp.int32, (8, BLOCK), 0)

    def merge(first, second, bit):
        if second is None:
            return first + pltpu.roll(first, bit, 0)
        low = (sub & bit) == 0
        return jnp.where(low, first, second) + pltpu.roll(jnp.where(low, second, first), bit, 0)

    pairs = [merge(terms[0], terms[1], 1), merge(terms[2], terms[3], 1), merge(terms[4], terms[5], 1)]
    return merge(merge(pairs[0], pairs[1], 2), merge(pairs[2], None, 2), 4)


def pick_lanes(rows, lanes):
    numbers = lax.GatherDimensionNumbers(
        offset_dims=(), collapsed_slice_dims=(1,), start_index_map=(1,),
        operand_batching_dims=(0,), start_indices_batching_dims=(0,),
    )
    return lax.gather(rows, lanes[:, :, None], numbers, (1, 1), mode=lax.GatherScatterMode.PROMISE_IN_BOUNDS)


def kernel(
    vel_h, pos_h, im_h, ii_h, nrm_h, lo_h, lt_h, bias_h, mass_h, pb_h, lane_h, cnt_h, gb_h,
    vout, pout,
    pos, im, ii, raw, slots, raw_lane, lane, cnt, bodies, vin,
    ext0, ext1, ext2, send, tmp, got, pb, gb, entries, ranks, tables, block_of, send_rows, place_row, rows_of,
    in_sem, send_sem, recv_sem,
):
    gx, gy, gz = lax.axis_index("gx"), lax.axis_index("gy"), lax.axis_index("gz")
    nx, ny, nz = lax.axis_size("gx"), lax.axis_size("gy"), lax.axis_size("gz")
    near = [
        ((gx + nx - 1) % nx, gy, gz), ((gx + 1) % nx, gy, gz),
        (gx, (gy + ny - 1) % ny, gz), (gx, (gy + 1) % ny, gz),
        (gx, gy, (gz + nz - 1) % nz), (gx, gy, (gz + 1) % nz),
    ]
    exts = [ext0, ext1, ext2]
    own, inv = bodies.at[0], bodies.at[1]
    nrm, co, ct = (slots.at[pl.ds(first, 3)] for first in (NORMAL, OWN_CROSS, OTHER_CROSS))
    base, bias, mass = (slots.at[which] for which in (BASE, BIAS, MASS))

    loads = [
        pltpu.make_async_copy(s, d, in_sem.at[i])
        for i, (s, d) in enumerate([
            (gb_h, gb), (vel_h, vin), (pb_h, pb), (nrm_h, raw.at[pl.ds(0, 3)]), (lo_h, raw.at[pl.ds(3, 3)]), (lt_h, raw.at[pl.ds(6, 3)]), (bias_h, raw.at[9]),
            (mass_h, raw.at[10]), (cnt_h, cnt), (im_h, im), (ii_h, ii), (lane_h, raw_lane), (pos_h, pos),
        ])
    ]
    for load in loads[:3]:
        load.start()
    barrier = pltpu.get_barrier_semaphore()
    for device in near:
        pl.semaphore_signal(barrier, inc=1, device_id=device, device_id_type=MESH)
    for load in loads[3:]:
        load.start()

    def column(b):
        return pl.ds(pl.multiple_of(b * BLOCK, BLOCK), BLOCK)

    def loop(count, body, unroll=UNROLL):
        def step(i, carry):
            for u in range(unroll):
                body(i * unroll + u, u)
            return carry
        lax.fori_loop(0, count // unroll, step, 0)

    far_x = gx % 2
    far_y = jnp.where(gy % ROW == 0, 2, 3)
    far_x_near = (jnp.where(far_x == 0, near[0][0], near[1][0]), gy, gz)
    pair_near = (jnp.where(far_x == 0, near[1][0], near[0][0]), gy, gz)
    far_y_near = (gx, jnp.where(far_y == 2, near[2][1], near[3][1]), gz)
    short_y_near = (gx, jnp.where(far_y == 2, near[3][1], near[2][1]), gz)
    first_face = [(far_x, far_x_near)]
    second_face = [(far_y, far_y_near)]
    other_faces = [(4, near[4]), (5, near[5]), (5 - far_y, short_y_near), (1 - far_x, pair_near)]

    def face_copy(round_number, face, device):
        region = face + 1 - 2 * (face % 2)
        return pltpu.make_async_remote_copy(
            src_ref=send.at[round_number, pl.ds(face * FACE_ROWS, FACE_ROWS)],
            dst_ref=exts[round_number].at[pl.ds((BLK + region * GHOST) * 6, FACE_ROWS)],
            send_sem=send_sem.at[round_number, face],
            recv_sem=recv_sem.at[round_number, face],
            device_id=device,
            device_id_type=MESH,
        )

    def receive(round_number):
        for face in range(6):
            face_copy(round_number, face, near[face]).wait()

    def start_faces(round_number, faces):
        for face, device in faces:
            face_copy(round_number, face, device).start()

    def send_faces(round_number, faces):
        def body(g, u):
            for face, _ in faces:
                row = send_rows[face * GHOST + g]
                send[round_number, pl.ds(face * FACE_ROWS + g * 6, 6), :] = own[pl.ds(row, 6), :]
        loop(GHOST, body, 4)
        start_faces(round_number, faces)

    loads[0].wait()
    loads[1].wait()

    def pack(g, u):
        for face in range(6):
            send[0, pl.ds(face * FACE_ROWS + g * 6, 6), :] = vin[:, pl.ds(gb[face, g] * BLOCK, BLOCK)]
    loop(GHOST, pack)
    pl.semaphore_wait(barrier, 6)
    start_faces(0, first_face + second_face + other_faces)

    loads[2].wait()
    down = lax.broadcasted_iota(jnp.int32, (BLK, BLK), 0)
    across = lax.broadcasted_iota(jnp.int32, (BLK, BLK), 1)
    sublane = lax.broadcasted_iota(jnp.int32, (8, BLK), 0)
    number = lax.broadcasted_iota(jnp.int32, (8, BLK), 1)
    found = jnp.zeros((8, BLK), jnp.int32)
    for face in range(6):
        row = jnp.zeros((8, BLK), jnp.int32)
        for g in range(GHOST):
            row = jnp.where(number == g, gb[face, g], row)
        found = jnp.where(sublane == face, row, found)
    entries[...] = found

    def in_face(face):
        found = jnp.broadcast_to(entries[pl.ds(face, 1), :], (BLK, BLK)) == down
        return jnp.sum(jnp.where(found & (across < GHOST), 1, 0), axis=1, keepdims=True) > 0

    def to_row(column):
        return jnp.sum(jnp.where(down == across, column, 0), axis=0, keepdims=True)

    def to_column(row):
        return jnp.sum(jnp.where(down == across, row, 0), axis=1, keepdims=True)

    key = jnp.where(in_face(far_x), 0, jnp.where(in_face(far_y), BLK, 2 * BLK)) + down[:, :1]
    place_of = jnp.sum(jnp.where(key < to_row(key), 1, 0), axis=0, keepdims=True)
    block_at = jnp.sum(jnp.where(to_column(place_of) == across, down, 0), axis=0, keepdims=True)
    place_of, block_at = (jnp.broadcast_to(jnp.clip(row, 0, BLK - 1), (8, BLK)) for row in (place_of, block_at))
    partner = pick_lanes(pb[...], block_at)
    partner_place = pick_lanes(place_of, jnp.minimum(partner, BLK - 1))
    ranks[pl.ds(0, 8), :] = 6 * jnp.where(partner < BLK, partner_place, partner)
    ranks[pl.ds(SEND_ROW, 8), :] = pick_lanes(place_of, entries[...])
    ranks[pl.ds(BLOCK_AT, 8), :] = block_at
    ranks[pl.ds(PLACE_OF, 8), :] = place_of
    to_scalars = pltpu.make_async_copy(ranks, tables, in_sem.at[0])
    to_scalars.start()
    to_scalars.wait()

    def orders(b, u):
        block_of[b] = tables[BLOCK_AT, b] & (BLK - 1)
    loop(BLK, orders)

    def entry_rows(g, u):
        for face in range(6):
            send_rows[face * GHOST + g] = (tables[SEND_ROW + face, g] & (BLK - 1)) * 8
    loop(GHOST, entry_rows)


    def unpack(i, u):
        rows = vin[:, pl.ds(block_of[i] * BLOCK, BLOCK)]
        own[pl.ds(pl.multiple_of(i * 8, 8), 6), :] = rows
        ext0[pl.ds(i * 6, 6), :] = rows
    loop(BLK, unpack)


    for load in loads[3:]:
        load.wait()

    slot_index = lax.broadcasted_iota(jnp.int32, (K, BLOCK), 0)

    def base_of(b, n, c_own, own_rows, total):
        for c in range(3):
            total = total - n[c] * own_rows(c)
            total = total - c_own[c] * own_rows(c + 3)
        base[:, column(b)] = total

    def cross(first, second):
        return [
            first[1] * second[2] - first[2] * second[1],
            first[2] * second[0] - first[0] * second[2],
            first[0] * second[1] - first[1] * second[0],
        ]

    def prepare(i, u):
        b = block_of[i]
        cols = column(i)
        source = [raw[c, :, pl.ds(b * BLOCK, BLOCK)] for c in range(11)]
        n = source[:3]
        c_own = cross([source[3 + c] for c in range(3)], n)
        c_other = cross([source[6 + c] for c in range(3)], n)
        target = slots.at[:, :, cols]
        for c in range(3):
            target[NORMAL + c] = n[c]
            target[OWN_CROSS + c] = c_own[c]
            target[OTHER_CROSS + c] = c_other[c]
        lane[:, cols] = raw_lane[:, pl.ds(b * BLOCK, BLOCK)]
        live = slot_index < jnp.broadcast_to(cnt[pl.ds(b, 1), :], (K, BLOCK))
        target[MASS] = jnp.where(live, -RELAXATION * source[10], 0.0)
        target[BIAS] = source[9]
        row = pl.multiple_of(i * 8, 8)
        inv[pl.ds(row, 3), :] = jnp.broadcast_to(im[pl.ds(b, 1), :], (3, BLOCK))
        inv[pl.ds(row + 3, 3), :] = ii[:, pl.ds(b * BLOCK, BLOCK)]
        base_of(i, n, c_own, lambda c: jnp.broadcast_to(own[pl.ds(row + c, 1), :], (K, BLOCK)), source[9])
    loop(BLK, prepare, 2)

    def scalars(i, u):
        place_row[i] = (tables[PLACE_OF, i] & (BLK - 1)) * 8
        for k in range(K):
            rows_of[i * K + k] = tables[k, i] & (TABLE_ROWS - 1)
    loop(BLK, scalars, 2)

    for it in range(ITERS):
        ext = exts[it]
        receive(it)
        last = it == ITERS - 1

        def gather(rows_at):
            for u, rows in enumerate(rows_at):
                for k in range(K):
                    tmp[pl.ds((u * K + k) * 9, 8), :] = ext[pl.ds(rows[k], 8), :]

        def permute(lanes_of):
            for u, lanes in enumerate(lanes_of):
                for c in range(6):
                    rows = tmp[pl.ds(u * 72 + c, 8, stride=9), :]
                    got[pl.ds((u * 6 + c) * 8, 8), :] = pick_lanes(rows, lanes)

        def impulse_and_moved(u, plane, own_b, inv_b):
            normal = [plane(NORMAL + c) for c in range(3)]
            terms = [(normal[c] if c < 3 else plane(OTHER_CROSS + c - 3)) * got[pl.ds((u * 6 + c) * 8, 8), :] for c in range(6)]
            total = ((terms[0] + terms[1]) + (terms[2] + terms[3])) + ((terms[4] + terms[5]) + plane(BASE))
            step = plane(MASS) * total
            if it == 0:
                new = jnp.maximum(step, 0.0)
                change = new
            else:
                old = plane(IMPULSE)
                new = jnp.maximum(old + step, 0.0)
                change = new - old
            sums = slot_sums([change * (normal[c] if c < 3 else plane(OWN_CROSS + c - 3)) for c in range(6)])
            return new, (own_b - inv_b * sums)[:6]

        def wide(i):
            return pl.ds(pl.multiple_of(i * (GROUP * BLOCK), GROUP * BLOCK), GROUP * BLOCK)

        def rows_at(i):
            rows = rows_of.at[pl.ds(i * (GROUP * K), GROUP * K)]
            return [[rows[u * K + k] for k in range(K)] for u in range(GROUP)]

        def lanes_at(i):
            lane_g = lane.at[:, wide(i)]
            return [lane_g[:, pl.ds(u * BLOCK, BLOCK)] for u in range(GROUP)]

        def update(i):
            slots_g = slots.at[:, :, wide(i)]
            bodies_g = bodies.at[:, pl.ds(pl.multiple_of(i * (GROUP * 8), GROUP * 8), GROUP * 8)]
            if not last:
                ext_g = exts[it + 1].at[pl.ds(pl.multiple_of(i * (GROUP * 6), GROUP * 6), GROUP * 6)]
            for u in range(GROUP):
                cols, row = pl.ds(u * BLOCK, BLOCK), pl.ds(u * 8, 8)
                new, moved = impulse_and_moved(u, lambda p: slots_g[p, :, cols], bodies_g[0, row, :], bodies_g[1, row, :])
                bodies_g[0, pl.ds(u * 8, 6), :] = moved
                if not last:
                    slots_g[IMPULSE, :, cols] = new
                    ext_g[pl.ds(u * 6, 6), :] = moved

        groups = BLK // GROUP

        def stages(i, carry):
            update(i)
            permute(lanes_at(jnp.minimum(i + 1, groups - 1)))
            gather(rows_at(jnp.minimum(i + 2, groups - 1)))
            return carry

        gather(rows_at(0))
        permute(lanes_at(0))
        gather(rows_at(1))
        if last:
            lax.fori_loop(0, groups, stages, 0)

            def finished(b, u):
                cols = column(b)
                moved = own[pl.ds(place_row[b], 6), :]
                vout[:, cols] = moved
                pout[:, cols] = pos[:, cols] + TIME_STEP * moved[:3]
            loop(BLK, finished)
        else:
            done = 0
            for blocks, faces in ((GHOST, first_face), (2 * GHOST, second_face), (BLK, other_faces)):
                until = -(-blocks // GROUP)
                lax.fori_loop(done, until, stages, 0)
                send_faces(it + 1, faces)
                done = until

            def rebase(b, u):
                cols = column(b)
                row = pl.multiple_of(b * 8, 8)
                base_of(
                    b, [nrm[c, :, cols] for c in range(3)], [co[c, :, cols] for c in range(3)],
                    lambda c: jnp.broadcast_to(own[pl.ds(row + c, 1), :], (K, BLOCK)), bias[:, cols],
                )
            loop(BLK, rebase)


def finish(moved, placed, vel_out, pos_out, sems):
    writes = [pltpu.make_async_copy(moved, vel_out, sems.at[0]), pltpu.make_async_copy(placed, pos_out, sems.at[1])]
    for write in writes:
        write.start()
    for write in writes:
        write.wait()


def per_device(
    velocity, positions, inverse_mass, inverse_inertia, normals, lever_own, lever_other, speed_bias, contact_mass,
    partner_block, partner_lane, slot_counts, ghost_blocks,
):
    bodies = BLK * BLOCK
    table = pltpu.VMEM((TABLE_ROWS + 8, BLOCK), jnp.float32)
    hbm = pl.BlockSpec(memory_space=pl.ANY)
    vmem = pl.BlockSpec(memory_space=pltpu.VMEM)
    moved, placed = pl.pallas_call(
        kernel,
        out_shape=(pltpu.VMEM((6, bodies), jnp.float32), pltpu.VMEM((3, bodies), jnp.float32)),
        in_specs=[hbm] * 13,
        out_specs=(vmem, vmem),
        scratch_shapes=[
            pltpu.VMEM((3, bodies), jnp.float32),
            pltpu.VMEM((BLK, BLOCK), jnp.float32),
            pltpu.VMEM((3, bodies), jnp.float32),
            pltpu.VMEM((11, K, bodies), jnp.float32),
            pltpu.VMEM((PLANES, K, bodies), jnp.float32),
            pltpu.VMEM((K, bodies), jnp.int32),
            pltpu.VMEM((K, bodies), jnp.int32),
            pltpu.VMEM((BLK, BLOCK), jnp.int32),
            pltpu.VMEM((2, BLK * 8, BLOCK), jnp.float32),
            pltpu.VMEM((6, bodies), jnp.float32),
            table, table, table,
            pltpu.VMEM((ITERS, 6 * FACE_ROWS, BLOCK), jnp.float32),
            pltpu.VMEM((GROUP * 72 + 16, BLOCK), jnp.float32),
            pltpu.VMEM((GROUP * 48, BLOCK), jnp.float32),
            pltpu.VMEM((K, BLK), jnp.int32),
            pltpu.SMEM((6, GHOST), jnp.int32),
            pltpu.VMEM((8, BLK), jnp.int32),
            pltpu.VMEM((32, BLK), jnp.int32),
            pltpu.SMEM((32, BLK), jnp.int32),
            pltpu.SMEM((BLK,), jnp.int32),
            pltpu.SMEM((6 * GHOST,), jnp.int32),
            pltpu.SMEM((BLK,), jnp.int32),
            pltpu.SMEM((BLK * K,), jnp.int32),
            pltpu.SemaphoreType.DMA((13,)),
            pltpu.SemaphoreType.DMA((ITERS, 6)),
            pltpu.SemaphoreType.DMA((ITERS, 6)),
        ],
        compiler_params=pltpu.CompilerParams(collective_id=0, has_side_effects=True),
    )(
        velocity, positions, inverse_mass.reshape(BLK, BLOCK), inverse_inertia, normals, lever_own, lever_other,
        speed_bias, contact_mass, partner_block, partner_lane, slot_counts.reshape(BLK, BLOCK), ghost_blocks,
    )
    return pl.pallas_call(
        finish,
        out_shape=(
            jax.ShapeDtypeStruct((6, bodies), jnp.float32),
            jax.ShapeDtypeStruct((3, bodies), jnp.float32),
        ),
        in_specs=[vmem, vmem],
        out_specs=(hbm, hbm),
        scratch_shapes=[pltpu.SemaphoreType.DMA((2,))],
    )(pltpu.with_memory_space_constraint(moved, pltpu.VMEM), pltpu.with_memory_space_constraint(placed, pltpu.VMEM))


def solution(mesh):
    every = ("gx", "gy", "gz")
    flat, wide, deep = P(every), P(None, every), P(None, None, every)
    return jax.shard_map(
        per_device,
        mesh=mesh,
        in_specs=(wide, wide, flat, wide, deep, deep, deep, wide, wide, wide, wide, flat, wide),
        out_specs=(wide, wide),
        check_vma=False,
    )
```

```python
import functools

import jax
import jax.numpy as jnp
from jax import lax
from jax.experimental import pallas as pl
from jax.experimental.pallas import tpu as pltpu
from jax.sharding import PartitionSpec as P

BLOCK = 128
BLK = 128
K = 8
GHOST = 40
ITERS = 3
EXT = BLK + 6 * GHOST
FACE_ROWS = GHOST * 6
TABLE_ROWS = 4096
RELAXATION = 0.25
TIME_STEP = 1.0 / 60.0
MESH = pl.DeviceIdType.MESH
UNROLL = 4
GROUP = 16
SEND_ROW, BLOCK_AT, PLACE_OF = 8, 16, 24
NORMAL, OWN_CROSS, OTHER_CROSS, BASE, BIAS, MASS, IMPULSE, PLANES = 0, 3, 6, 9, 10, 11, 12, 13
ROW = 4


def slot_sums(terms):
    sub = lax.broadcasted_iota(jnp.int32, (8, BLOCK), 0)

    def merge(first, second, bit):
        if second is None:
            return first + pltpu.roll(first, bit, 0)
        low = (sub & bit) == 0
        return jnp.where(low, first, second) + pltpu.roll(jnp.where(low, second, first), bit, 0)

    pairs = [merge(terms[0], terms[1], 1), merge(terms[2], terms[3], 1), merge(terms[4], terms[5], 1)]
    return merge(merge(pairs[0], pairs[1], 2), merge(pairs[2], None, 2), 4)


def pick_lanes(rows, lanes):
    numbers = lax.GatherDimensionNumbers(
        offset_dims=(), collapsed_slice_dims=(1,), start_index_map=(1,),
        operand_batching_dims=(0,), start_indices_batching_dims=(0,),
    )
    return lax.gather(rows, lanes[:, :, None], numbers, (1, 1), mode=lax.GatherScatterMode.PROMISE_IN_BOUNDS)


def kernel(
    vel_h, pos_h, im_h, ii_h, nrm_h, lo_h, lt_h, bias_h, mass_h, pb_h, lane_h, cnt_h, gb_h,
    vout, pout,
    pos, im, ii, raw, slots, raw_lane, lane, cnt, bodies, vin,
    ext0, ext1, ext2, send, tmp, got, pb, gb, entries, ranks, tables, block_of, send_rows, place_row, rows_of,
    in_sem, send_sem, recv_sem,
):
    gx, gy, gz = lax.axis_index("gx"), lax.axis_index("gy"), lax.axis_index("gz")
    nx, ny, nz = lax.axis_size("gx"), lax.axis_size("gy"), lax.axis_size("gz")
    near = [
        ((gx + nx - 1) % nx, gy, gz), ((gx + 1) % nx, gy, gz),
        (gx, (gy + ny - 1) % ny, gz), (gx, (gy + 1) % ny, gz),
        (gx, gy, (gz + nz - 1) % nz), (gx, gy, (gz + 1) % nz),
    ]
    exts = [ext0, ext1, ext2]
    own, inv = bodies.at[0], bodies.at[1]
    nrm, co, ct = (slots.at[pl.ds(first, 3)] for first in (NORMAL, OWN_CROSS, OTHER_CROSS))
    base, bias, mass = (slots.at[which] for which in (BASE, BIAS, MASS))

    loads = [
        pltpu.make_async_copy(s, d, in_sem.at[i])
        for i, (s, d) in enumerate([
            (gb_h, gb), (vel_h, vin), (pb_h, pb), (nrm_h, raw.at[pl.ds(0, 3)]), (lo_h, raw.at[pl.ds(3, 3)]), (lt_h, raw.at[pl.ds(6, 3)]), (bias_h, raw.at[9]),
            (mass_h, raw.at[10]), (cnt_h, cnt), (im_h, im), (ii_h, ii), (lane_h, raw_lane), (pos_h, pos),
        ])
    ]
    for load in loads[:3]:
        load.start()
    barrier = pltpu.get_barrier_semaphore()
    for device in near:
        pl.semaphore_signal(barrier, inc=1, device_id=device, device_id_type=MESH)
    for load in loads[3:]:
        load.start()

    def column(b):
        return pl.ds(pl.multiple_of(b * BLOCK, BLOCK), BLOCK)

    def loop(count, body, unroll=UNROLL):
        def step(i, carry):
            for u in range(unroll):
                body(i * unroll + u, u)
            return carry
        lax.fori_loop(0, count // unroll, step, 0)

    far_x = gx % 2
    far_y = jnp.where(gy % ROW == 0, 2, 3)
    far_x_near = (jnp.where(far_x == 0, near[0][0], near[1][0]), gy, gz)
    pair_near = (jnp.where(far_x == 0, near[1][0], near[0][0]), gy, gz)
    far_y_near = (gx, jnp.where(far_y == 2, near[2][1], near[3][1]), gz)
    short_y_near = (gx, jnp.where(far_y == 2, near[3][1], near[2][1]), gz)
    first_face = [(far_x, far_x_near)]
    second_face = [(far_y, far_y_near)]
    other_faces = [(4, near[4]), (5, near[5]), (5 - far_y, short_y_near), (1 - far_x, pair_near)]

    def face_copy(round_number, face, device):
        region = face + 1 - 2 * (face % 2)
        return pltpu.make_async_remote_copy(
            src_ref=send.at[round_number, pl.ds(face * FACE_ROWS, FACE_ROWS)],
            dst_ref=exts[round_number].at[pl.ds((BLK + region * GHOST) * 6, FACE_ROWS)],
            send_sem=send_sem.at[round_number, face],
            recv_sem=recv_sem.at[round_number, face],
            device_id=device,
            device_id_type=MESH,
        )

    def receive(round_number):
        for face in range(6):
            face_copy(round_number, face, near[face]).wait()

    def start_faces(round_number, faces):
        for face, device in faces:
            face_copy(round_number, face, device).start()

    def send_faces(round_number, faces):
        def body(g, u):
            for face, _ in faces:
                row = send_rows[face * GHOST + g]
                send[round_number, pl.ds(face * FACE_ROWS + g * 6, 6), :] = own[pl.ds(row, 6), :]
        loop(GHOST, body, 20)
        start_faces(round_number, faces)

    loads[0].wait()
    loads[1].wait()

    def pack(g, u):
        for face in range(6):
            send[0, pl.ds(face * FACE_ROWS + g * 6, 6), :] = vin[:, pl.ds(gb[face, g] * BLOCK, BLOCK)]
    loop(GHOST, pack)
    pl.semaphore_wait(barrier, 6)
    start_faces(0, first_face + second_face + other_faces)

    loads[2].wait()
    down = lax.broadcasted_iota(jnp.int32, (BLK, BLK), 0)
    across = lax.broadcasted_iota(jnp.int32, (BLK, BLK), 1)
    sublane = lax.broadcasted_iota(jnp.int32, (8, BLK), 0)
    number = lax.broadcasted_iota(jnp.int32, (8, BLK), 1)
    found = jnp.zeros((8, BLK), jnp.int32)
    for face in range(6):
        row = jnp.zeros((8, BLK), jnp.int32)
        for g in range(GHOST):
            row = jnp.where(number == g, gb[face, g], row)
        found = jnp.where(sublane == face, row, found)
    entries[...] = found

    def in_face(face):
        found = jnp.broadcast_to(entries[pl.ds(face, 1), :], (BLK, BLK)) == down
        return jnp.sum(jnp.where(found & (across < GHOST), 1, 0), axis=1, keepdims=True) > 0

    def to_row(column):
        return jnp.sum(jnp.where(down == across, column, 0), axis=0, keepdims=True)

    def to_column(row):
        return jnp.sum(jnp.where(down == across, row, 0), axis=1, keepdims=True)

    key = jnp.where(in_face(far_x), 0, jnp.where(in_face(far_y), BLK, 2 * BLK)) + down[:, :1]
    place_of = jnp.sum(jnp.where(key < to_row(key), 1, 0), axis=0, keepdims=True)
    block_at = jnp.sum(jnp.where(to_column(place_of) == across, down, 0), axis=0, keepdims=True)
    place_of, block_at = (jnp.broadcast_to(jnp.clip(row, 0, BLK - 1), (8, BLK)) for row in (place_of, block_at))
    partner = pick_lanes(pb[...], block_at)
    partner_place = pick_lanes(place_of, jnp.minimum(partner, BLK - 1))
    ranks[pl.ds(0, 8), :] = 6 * jnp.where(partner < BLK, partner_place, partner)
    ranks[pl.ds(SEND_ROW, 8), :] = pick_lanes(place_of, entries[...])
    ranks[pl.ds(BLOCK_AT, 8), :] = block_at
    ranks[pl.ds(PLACE_OF, 8), :] = place_of
    to_scalars = pltpu.make_async_copy(ranks, tables, in_sem.at[0])
    to_scalars.start()
    to_scalars.wait()

    def orders(b, u):
        block_of[b] = tables[BLOCK_AT, b] & (BLK - 1)
    loop(BLK, orders)

    def entry_rows(g, u):
        for face in range(6):
            send_rows[face * GHOST + g] = (tables[SEND_ROW + face, g] & (BLK - 1)) * 8
    loop(GHOST, entry_rows)


    def unpack(i, u):
        rows = vin[:, pl.ds(block_of[i] * BLOCK, BLOCK)]
        own[pl.ds(pl.multiple_of(i * 8, 8), 6), :] = rows
        ext0[pl.ds(i * 6, 6), :] = rows
    loop(BLK, unpack)


    for load in loads[3:]:
        load.wait()

    slot_index = lax.broadcasted_iota(jnp.int32, (K, BLOCK), 0)

    def base_of(b, n, c_own, own_rows, total):
        for c in range(3):
            total = total - n[c] * own_rows(c)
            total = total - c_own[c] * own_rows(c + 3)
        base[:, column(b)] = total

    def cross(first, second):
        return [
            first[1] * second[2] - first[2] * second[1],
            first[2] * second[0] - first[0] * second[2],
            first[0] * second[1] - first[1] * second[0],
        ]

    def prepare(i, u):
        b = block_of[i]
        cols = column(i)
        source = [raw[c, :, pl.ds(b * BLOCK, BLOCK)] for c in range(11)]
        n = source[:3]
        c_own = cross([source[3 + c] for c in range(3)], n)
        c_other = cross([source[6 + c] for c in range(3)], n)
        target = slots.at[:, :, cols]
        for c in range(3):
            target[NORMAL + c] = n[c]
            target[OWN_CROSS + c] = c_own[c]
            target[OTHER_CROSS + c] = c_other[c]
        lane[:, cols] = raw_lane[:, pl.ds(b * BLOCK, BLOCK)]
        live = slot_index < jnp.broadcast_to(cnt[pl.ds(b, 1), :], (K, BLOCK))
        target[MASS] = jnp.where(live, -RELAXATION * source[10], 0.0)
        target[BIAS] = source[9]
        row = pl.multiple_of(i * 8, 8)
        inv[pl.ds(row, 3), :] = jnp.broadcast_to(im[pl.ds(b, 1), :], (3, BLOCK))
        inv[pl.ds(row + 3, 3), :] = ii[:, pl.ds(b * BLOCK, BLOCK)]
        base_of(i, n, c_own, lambda c: jnp.broadcast_to(own[pl.ds(row + c, 1), :], (K, BLOCK)), source[9])
    loop(BLK, prepare, 2)

    def scalars(i, u):
        place_row[i] = (tables[PLACE_OF, i] & (BLK - 1)) * 8
        for k in range(K):
            rows_of[i * K + k] = tables[k, i] & (TABLE_ROWS - 1)
    loop(BLK, scalars, 2)

    for it in range(ITERS):
        ext = exts[it]
        receive(it)
        last = it == ITERS - 1

        def gather(rows_at):
            for u, rows in enumerate(rows_at):
                for k in range(K):
                    tmp[pl.ds((u * K + k) * 9, 8), :] = ext[pl.ds(rows[k], 8), :]

        def permute(lanes_of):
            for u, lanes in enumerate(lanes_of):
                for c in range(6):
                    rows = tmp[pl.ds(u * 72 + c, 8, stride=9), :]
                    got[pl.ds((u * 6 + c) * 8, 8), :] = pick_lanes(rows, lanes)

        def impulse_and_moved(u, plane, own_b, inv_b):
            normal = [plane(NORMAL + c) for c in range(3)]
            terms = [(normal[c] if c < 3 else plane(OTHER_CROSS + c - 3)) * got[pl.ds((u * 6 + c) * 8, 8), :] for c in range(6)]
            total = ((terms[0] + terms[1]) + (terms[2] + terms[3])) + ((terms[4] + terms[5]) + plane(BASE))
            step = plane(MASS) * total
            if it == 0:
                new = jnp.maximum(step, 0.0)
                change = new
            else:
                old = plane(IMPULSE)
                new = jnp.maximum(old + step, 0.0)
                change = new - old
            sums = slot_sums([change * (normal[c] if c < 3 else plane(OWN_CROSS + c - 3)) for c in range(6)])
            return new, (own_b - inv_b * sums)[:6]

        def wide(i):
            return pl.ds(pl.multiple_of(i * (GROUP * BLOCK), GROUP * BLOCK), GROUP * BLOCK)

        def rows_at(i):
            rows = rows_of.at[pl.ds(i * (GROUP * K), GROUP * K)]
            return [[rows[u * K + k] for k in range(K)] for u in range(GROUP)]

        def lanes_at(i):
            lane_g = lane.at[:, wide(i)]
            return [lane_g[:, pl.ds(u * BLOCK, BLOCK)] for u in range(GROUP)]

        def update(i):
            slots_g = slots.at[:, :, wide(i)]
            bodies_g = bodies.at[:, pl.ds(pl.multiple_of(i * (GROUP * 8), GROUP * 8), GROUP * 8)]
            if not last:
                ext_g = exts[it + 1].at[pl.ds(pl.multiple_of(i * (GROUP * 6), GROUP * 6), GROUP * 6)]
            for u in range(GROUP):
                cols, row = pl.ds(u * BLOCK, BLOCK), pl.ds(u * 8, 8)
                new, moved = impulse_and_moved(u, lambda p: slots_g[p, :, cols], bodies_g[0, row, :], bodies_g[1, row, :])
                bodies_g[0, pl.ds(u * 8, 6), :] = moved
                if not last:
                    slots_g[IMPULSE, :, cols] = new
                    ext_g[pl.ds(u * 6, 6), :] = moved

        groups = BLK // GROUP

        def stages(i, carry):
            update(i)
            permute(lanes_at(jnp.minimum(i + 1, groups - 1)))
            gather(rows_at(jnp.minimum(i + 2, groups - 1)))
            return carry

        gather(rows_at(0))
        permute(lanes_at(0))
        gather(rows_at(1))
        if last:
            lax.fori_loop(0, groups, stages, 0)

            def finished(b, u):
                cols = column(b)
                moved = own[pl.ds(place_row[b], 6), :]
                vout[:, cols] = moved
                pout[:, cols] = pos[:, cols] + TIME_STEP * moved[:3]
            loop(BLK, finished, 32)
        else:
            done = 0
            for blocks, faces in ((GHOST, first_face), (2 * GHOST, second_face), (BLK, other_faces)):
                until = -(-blocks // GROUP)
                lax.fori_loop(done, until, stages, 0)
                send_faces(it + 1, faces)
                done = until

            def rebase(b, u):
                cols = column(b)
                row = pl.multiple_of(b * 8, 8)
                base_of(
                    b, [nrm[c, :, cols] for c in range(3)], [co[c, :, cols] for c in range(3)],
                    lambda c: jnp.broadcast_to(own[pl.ds(row + c, 1), :], (K, BLOCK)), bias[:, cols],
                )
            loop(BLK, rebase)


def finish(moved, placed, vel_out, pos_out, sems):
    writes = [pltpu.make_async_copy(moved, vel_out, sems.at[0]), pltpu.make_async_copy(placed, pos_out, sems.at[1])]
    for write in writes:
        write.start()
    for write in writes:
        write.wait()


def per_device(
    velocity, positions, inverse_mass, inverse_inertia, normals, lever_own, lever_other, speed_bias, contact_mass,
    partner_block, partner_lane, slot_counts, ghost_blocks,
):
    bodies = BLK * BLOCK
    table = pltpu.VMEM((TABLE_ROWS + 8, BLOCK), jnp.float32)
    hbm = pl.BlockSpec(memory_space=pl.ANY)
    vmem = pl.BlockSpec(memory_space=pltpu.VMEM)
    moved, placed = pl.pallas_call(
        kernel,
        out_shape=(pltpu.VMEM((6, bodies), jnp.float32), pltpu.VMEM((3, bodies), jnp.float32)),
        in_specs=[hbm] * 13,
        out_specs=(vmem, vmem),
        scratch_shapes=[
            pltpu.VMEM((3, bodies), jnp.float32),
            pltpu.VMEM((BLK, BLOCK), jnp.float32),
            pltpu.VMEM((3, bodies), jnp.float32),
            pltpu.VMEM((11, K, bodies), jnp.float32),
            pltpu.VMEM((PLANES, K, bodies), jnp.float32),
            pltpu.VMEM((K, bodies), jnp.int32),
            pltpu.VMEM((K, bodies), jnp.int32),
            pltpu.VMEM((BLK, BLOCK), jnp.int32),
            pltpu.VMEM((2, BLK * 8, BLOCK), jnp.float32),
            pltpu.VMEM((6, bodies), jnp.float32),
            table, table, table,
            pltpu.VMEM((ITERS, 6 * FACE_ROWS, BLOCK), jnp.float32),
            pltpu.VMEM((GROUP * 72 + 16, BLOCK), jnp.float32),
            pltpu.VMEM((GROUP * 48, BLOCK), jnp.float32),
            pltpu.VMEM((K, BLK), jnp.int32),
            pltpu.SMEM((6, GHOST), jnp.int32),
            pltpu.VMEM((8, BLK), jnp.int32),
            pltpu.VMEM((32, BLK), jnp.int32),
            pltpu.SMEM((32, BLK), jnp.int32),
            pltpu.SMEM((BLK,), jnp.int32),
            pltpu.SMEM((6 * GHOST,), jnp.int32),
            pltpu.SMEM((BLK,), jnp.int32),
            pltpu.SMEM((BLK * K,), jnp.int32),
            pltpu.SemaphoreType.DMA((13,)),
            pltpu.SemaphoreType.DMA((ITERS, 6)),
            pltpu.SemaphoreType.DMA((ITERS, 6)),
        ],
        compiler_params=pltpu.CompilerParams(collective_id=0, has_side_effects=True),
    )(
        velocity, positions, inverse_mass.reshape(BLK, BLOCK), inverse_inertia, normals, lever_own, lever_other,
        speed_bias, contact_mass, partner_block, partner_lane, slot_counts.reshape(BLK, BLOCK), ghost_blocks,
    )
    return pl.pallas_call(
        finish,
        out_shape=(
            jax.ShapeDtypeStruct((6, bodies), jnp.float32),
            jax.ShapeDtypeStruct((3, bodies), jnp.float32),
        ),
        in_specs=[vmem, vmem],
        out_specs=(hbm, hbm),
        scratch_shapes=[pltpu.SemaphoreType.DMA((2,))],
    )(pltpu.with_memory_space_constraint(moved, pltpu.VMEM), pltpu.with_memory_space_constraint(placed, pltpu.VMEM))


def solution(mesh):
    every = ("gx", "gy", "gz")
    flat, wide, deep = P(every), P(None, every), P(None, None, every)
    return jax.shard_map(
        per_device,
        mesh=mesh,
        in_specs=(wide, wide, flat, wide, deep, deep, deep, wide, wide, wide, wide, flat, wide),
        out_specs=(wide, wide),
        check_vma=False,
    )
```

```python
import functools

import jax
import jax.numpy as jnp
from jax import lax
from jax.experimental import pallas as pl
from jax.experimental.pallas import tpu as pltpu
from jax.sharding import PartitionSpec as P

BLOCK = 128
BLK = 128
K = 8
GHOST = 40
ITERS = 3
EXT = BLK + 6 * GHOST
FACE_ROWS = GHOST * 6
TABLE_ROWS = 4096
RELAXATION = 0.25
TIME_STEP = 1.0 / 60.0
MESH = pl.DeviceIdType.MESH
UNROLL = 4
GROUP = 16
LAST_GROUP = 32
SEND_ROW, BLOCK_AT, PLACE_OF = 8, 16, 24
NORMAL, OWN_CROSS, OTHER_CROSS, BASE, BIAS, MASS, IMPULSE, PLANES = 0, 3, 6, 9, 10, 11, 12, 13
ROW = 4


def slot_sums(terms):
    sub = lax.broadcasted_iota(jnp.int32, (8, BLOCK), 0)

    def merge(first, second, bit):
        if second is None:
            return first + pltpu.roll(first, bit, 0)
        low = (sub & bit) == 0
        return jnp.where(low, first, second) + pltpu.roll(jnp.where(low, second, first), bit, 0)

    pairs = [merge(terms[0], terms[1], 1), merge(terms[2], terms[3], 1), merge(terms[4], terms[5], 1)]
    return merge(merge(pairs[0], pairs[1], 2), merge(pairs[2], None, 2), 4)


def pick_lanes(rows, lanes):
    numbers = lax.GatherDimensionNumbers(
        offset_dims=(), collapsed_slice_dims=(1,), start_index_map=(1,),
        operand_batching_dims=(0,), start_indices_batching_dims=(0,),
    )
    return lax.gather(rows, lanes[:, :, None], numbers, (1, 1), mode=lax.GatherScatterMode.PROMISE_IN_BOUNDS)


def kernel(
    vel_h, pos_h, im_h, ii_h, nrm_h, lo_h, lt_h, bias_h, mass_h, pb_h, lane_h, cnt_h, gb_h,
    vout, pout,
    pos, im, ii, raw, slots, raw_lane, lane, cnt, bodies, vin,
    ext0, ext1, ext2, send, tmp, got, pb, gb, entries, ranks, tables, block_of, send_rows, place_row, rows_of,
    in_sem, send_sem, recv_sem,
):
    gx, gy, gz = lax.axis_index("gx"), lax.axis_index("gy"), lax.axis_index("gz")
    nx, ny, nz = lax.axis_size("gx"), lax.axis_size("gy"), lax.axis_size("gz")
    near = [
        ((gx + nx - 1) % nx, gy, gz), ((gx + 1) % nx, gy, gz),
        (gx, (gy + ny - 1) % ny, gz), (gx, (gy + 1) % ny, gz),
        (gx, gy, (gz + nz - 1) % nz), (gx, gy, (gz + 1) % nz),
    ]
    exts = [ext0, ext1, ext2]
    own, inv = bodies.at[0], bodies.at[1]
    nrm, co, ct = (slots.at[pl.ds(first, 3)] for first in (NORMAL, OWN_CROSS, OTHER_CROSS))
    base, bias, mass = (slots.at[which] for which in (BASE, BIAS, MASS))

    loads = [
        pltpu.make_async_copy(s, d, in_sem.at[i])
        for i, (s, d) in enumerate([
            (gb_h, gb), (vel_h, vin), (pb_h, pb), (nrm_h, raw.at[pl.ds(0, 3)]), (lo_h, raw.at[pl.ds(3, 3)]), (lt_h, raw.at[pl.ds(6, 3)]), (bias_h, raw.at[9]),
            (mass_h, raw.at[10]), (cnt_h, cnt), (im_h, im), (ii_h, ii), (lane_h, raw_lane), (pos_h, pos),
        ])
    ]
    for load in loads[:3]:
        load.start()
    barrier = pltpu.get_barrier_semaphore()
    for device in near:
        pl.semaphore_signal(barrier, inc=1, device_id=device, device_id_type=MESH)
    for load in loads[3:]:
        load.start()

    def column(b):
        return pl.ds(pl.multiple_of(b * BLOCK, BLOCK), BLOCK)

    def loop(count, body, unroll=UNROLL):
        def step(i, carry):
            for u in range(unroll):
                body(i * unroll + u, u)
            return carry
        lax.fori_loop(0, count // unroll, step, 0)

    far_x = gx % 2
    far_y = jnp.where(gy % ROW == 0, 2, 3)
    far_x_near = (jnp.where(far_x == 0, near[0][0], near[1][0]), gy, gz)
    pair_near = (jnp.where(far_x == 0, near[1][0], near[0][0]), gy, gz)
    far_y_near = (gx, jnp.where(far_y == 2, near[2][1], near[3][1]), gz)
    short_y_near = (gx, jnp.where(far_y == 2, near[3][1], near[2][1]), gz)
    first_face = [(far_x, far_x_near)]
    second_face = [(far_y, far_y_near)]
    other_faces = [(4, near[4]), (5, near[5]), (5 - far_y, short_y_near), (1 - far_x, pair_near)]

    def face_copy(round_number, face, device):
        region = face + 1 - 2 * (face % 2)
        return pltpu.make_async_remote_copy(
            src_ref=send.at[round_number, pl.ds(face * FACE_ROWS, FACE_ROWS)],
            dst_ref=exts[round_number].at[pl.ds((BLK + region * GHOST) * 6, FACE_ROWS)],
            send_sem=send_sem.at[round_number, face],
            recv_sem=recv_sem.at[round_number, face],
            device_id=device,
            device_id_type=MESH,
        )

    def receive(round_number):
        for face in range(6):
            face_copy(round_number, face, near[face]).wait()

    def start_faces(round_number, faces):
        for face, device in faces:
            face_copy(round_number, face, device).start()

    def send_faces(round_number, faces):
        def body(g, u):
            for face, _ in faces:
                row = send_rows[face * GHOST + g]
                send[round_number, pl.ds(face * FACE_ROWS + g * 6, 6), :] = own[pl.ds(row, 6), :]
        loop(GHOST, body, 20)
        start_faces(round_number, faces)

    loads[0].wait()
    loads[1].wait()

    def pack(g, u):
        for face in range(6):
            send[0, pl.ds(face * FACE_ROWS + g * 6, 6), :] = vin[:, pl.ds(gb[face, g] * BLOCK, BLOCK)]
    loop(GHOST, pack)
    pl.semaphore_wait(barrier, 6)
    start_faces(0, first_face + second_face + other_faces)

    loads[2].wait()
    down = lax.broadcasted_iota(jnp.int32, (BLK, BLK), 0)
    across = lax.broadcasted_iota(jnp.int32, (BLK, BLK), 1)
    sublane = lax.broadcasted_iota(jnp.int32, (8, BLK), 0)
    number = lax.broadcasted_iota(jnp.int32, (8, BLK), 1)
    found = jnp.zeros((8, BLK), jnp.int32)
    for face in range(6):
        row = jnp.zeros((8, BLK), jnp.int32)
        for g in range(GHOST):
            row = jnp.where(number == g, gb[face, g], row)
        found = jnp.where(sublane == face, row, found)
    entries[...] = found

    def in_face(face):
        found = jnp.broadcast_to(entries[pl.ds(face, 1), :], (BLK, BLK)) == down
        return jnp.sum(jnp.where(found & (across < GHOST), 1, 0), axis=1, keepdims=True) > 0

    def to_row(column):
        return jnp.sum(jnp.where(down == across, column, 0), axis=0, keepdims=True)

    def to_column(row):
        return jnp.sum(jnp.where(down == across, row, 0), axis=1, keepdims=True)

    key = jnp.where(in_face(far_x), 0, jnp.where(in_face(far_y), BLK, 2 * BLK)) + down[:, :1]
    place_of = jnp.sum(jnp.where(key < to_row(key), 1, 0), axis=0, keepdims=True)
    block_at = jnp.sum(jnp.where(to_column(place_of) == across, down, 0), axis=0, keepdims=True)
    place_of, block_at = (jnp.broadcast_to(jnp.clip(row, 0, BLK - 1), (8, BLK)) for row in (place_of, block_at))
    partner = pick_lanes(pb[...], block_at)
    partner_place = pick_lanes(place_of, jnp.minimum(partner, BLK - 1))
    ranks[pl.ds(0, 8), :] = 6 * jnp.where(partner < BLK, partner_place, partner)
    ranks[pl.ds(SEND_ROW, 8), :] = pick_lanes(place_of, entries[...])
    ranks[pl.ds(BLOCK_AT, 8), :] = block_at
    ranks[pl.ds(PLACE_OF, 8), :] = place_of
    to_scalars = pltpu.make_async_copy(ranks, tables, in_sem.at[0])
    to_scalars.start()
    to_scalars.wait()

    def orders(b, u):
        block_of[b] = tables[BLOCK_AT, b] & (BLK - 1)
    loop(BLK, orders)

    def entry_rows(g, u):
        for face in range(6):
            send_rows[face * GHOST + g] = (tables[SEND_ROW + face, g] & (BLK - 1)) * 8
    loop(GHOST, entry_rows)


    def unpack(i, u):
        rows = vin[:, pl.ds(block_of[i] * BLOCK, BLOCK)]
        own[pl.ds(pl.multiple_of(i * 8, 8), 6), :] = rows
        ext0[pl.ds(i * 6, 6), :] = rows
    loop(BLK, unpack)


    for load in loads[3:]:
        load.wait()

    slot_index = lax.broadcasted_iota(jnp.int32, (K, BLOCK), 0)

    def base_of(b, n, c_own, own_rows, total):
        for c in range(3):
            total = total - n[c] * own_rows(c)
            total = total - c_own[c] * own_rows(c + 3)
        base[:, column(b)] = total

    def cross(first, second):
        return [
            first[1] * second[2] - first[2] * second[1],
            first[2] * second[0] - first[0] * second[2],
            first[0] * second[1] - first[1] * second[0],
        ]

    def prepare(i, u):
        b = block_of[i]
        cols = column(i)
        source = [raw[c, :, pl.ds(b * BLOCK, BLOCK)] for c in range(11)]
        n = source[:3]
        c_own = cross([source[3 + c] for c in range(3)], n)
        c_other = cross([source[6 + c] for c in range(3)], n)
        target = slots.at[:, :, cols]
        for c in range(3):
            target[NORMAL + c] = n[c]
            target[OWN_CROSS + c] = c_own[c]
            target[OTHER_CROSS + c] = c_other[c]
        lane[:, cols] = raw_lane[:, pl.ds(b * BLOCK, BLOCK)]
        live = slot_index < jnp.broadcast_to(cnt[pl.ds(b, 1), :], (K, BLOCK))
        target[MASS] = jnp.where(live, -RELAXATION * source[10], 0.0)
        target[BIAS] = source[9]
        row = pl.multiple_of(i * 8, 8)
        inv[pl.ds(row, 3), :] = jnp.broadcast_to(im[pl.ds(b, 1), :], (3, BLOCK))
        inv[pl.ds(row + 3, 3), :] = ii[:, pl.ds(b * BLOCK, BLOCK)]
        base_of(i, n, c_own, lambda c: jnp.broadcast_to(own[pl.ds(row + c, 1), :], (K, BLOCK)), source[9])
    loop(BLK, prepare, 2)

    def scalars(i, u):
        place_row[i] = (tables[PLACE_OF, i] & (BLK - 1)) * 8
        for k in range(K):
            rows_of[i * K + k] = tables[k, i] & (TABLE_ROWS - 1)
    loop(BLK, scalars, 2)

    for it in range(ITERS):
        ext = exts[it]
        receive(it)
        last = it == ITERS - 1
        size = LAST_GROUP if last else GROUP

        def gather(rows_at):
            for u, rows in enumerate(rows_at):
                for k in range(K):
                    tmp[pl.ds((u * K + k) * 9, 8), :] = ext[pl.ds(rows[k], 8), :]

        def permute(lanes_of):
            for u, lanes in enumerate(lanes_of):
                for c in range(6):
                    rows = tmp[pl.ds(u * 72 + c, 8, stride=9), :]
                    got[pl.ds((u * 6 + c) * 8, 8), :] = pick_lanes(rows, lanes)

        def impulse_and_moved(u, plane, own_b, inv_b):
            normal = [plane(NORMAL + c) for c in range(3)]
            terms = [(normal[c] if c < 3 else plane(OTHER_CROSS + c - 3)) * got[pl.ds((u * 6 + c) * 8, 8), :] for c in range(6)]
            total = ((terms[0] + terms[1]) + (terms[2] + terms[3])) + ((terms[4] + terms[5]) + plane(BASE))
            step = plane(MASS) * total
            if it == 0:
                new = jnp.maximum(step, 0.0)
                change = new
            else:
                old = plane(IMPULSE)
                new = jnp.maximum(old + step, 0.0)
                change = new - old
            sums = slot_sums([change * (normal[c] if c < 3 else plane(OWN_CROSS + c - 3)) for c in range(6)])
            return new, (own_b - inv_b * sums)[:6]

        def wide(i):
            return pl.ds(pl.multiple_of(i * (size * BLOCK), size * BLOCK), size * BLOCK)

        def rows_at(i):
            rows = rows_of.at[pl.ds(i * (size * K), size * K)]
            return [[rows[u * K + k] for k in range(K)] for u in range(size)]

        def lanes_at(i):
            lane_g = lane.at[:, wide(i)]
            return [lane_g[:, pl.ds(u * BLOCK, BLOCK)] for u in range(size)]

        def update(i):
            slots_g = slots.at[:, :, wide(i)]
            bodies_g = bodies.at[:, pl.ds(pl.multiple_of(i * (size * 8), size * 8), size * 8)]
            if not last:
                ext_g = exts[it + 1].at[pl.ds(pl.multiple_of(i * (size * 6), size * 6), size * 6)]
            for u in range(size):
                cols, row = pl.ds(u * BLOCK, BLOCK), pl.ds(u * 8, 8)
                new, moved = impulse_and_moved(u, lambda p: slots_g[p, :, cols], bodies_g[0, row, :], bodies_g[1, row, :])
                bodies_g[0, pl.ds(u * 8, 6), :] = moved
                if not last:
                    slots_g[IMPULSE, :, cols] = new
                    ext_g[pl.ds(u * 6, 6), :] = moved

        groups = BLK // size

        def stages(i, carry):
            update(i)
            permute(lanes_at(jnp.minimum(i + 1, groups - 1)))
            gather(rows_at(jnp.minimum(i + 2, groups - 1)))
            return carry

        gather(rows_at(0))
        permute(lanes_at(0))
        gather(rows_at(1))
        if last:
            lax.fori_loop(0, groups, stages, 0)

            def finished(b, u):
                cols = column(b)
                moved = own[pl.ds(place_row[b], 6), :]
                vout[:, cols] = moved
                pout[:, cols] = pos[:, cols] + TIME_STEP * moved[:3]
            loop(BLK, finished, 32)
        else:
            done = 0
            for blocks, faces in ((GHOST, first_face), (2 * GHOST, second_face), (BLK, other_faces)):
                until = -(-blocks // size)
                lax.fori_loop(done, until, stages, 0)
                send_faces(it + 1, faces)
                done = until

            def rebase(b, u):
                cols = column(b)
                row = pl.multiple_of(b * 8, 8)
                base_of(
                    b, [nrm[c, :, cols] for c in range(3)], [co[c, :, cols] for c in range(3)],
                    lambda c: jnp.broadcast_to(own[pl.ds(row + c, 1), :], (K, BLOCK)), bias[:, cols],
                )
            loop(BLK, rebase)


def finish(moved, placed, vel_out, pos_out, sems):
    writes = [pltpu.make_async_copy(moved, vel_out, sems.at[0]), pltpu.make_async_copy(placed, pos_out, sems.at[1])]
    for write in writes:
        write.start()
    for write in writes:
        write.wait()


def per_device(
    velocity, positions, inverse_mass, inverse_inertia, normals, lever_own, lever_other, speed_bias, contact_mass,
    partner_block, partner_lane, slot_counts, ghost_blocks,
):
    bodies = BLK * BLOCK
    table = pltpu.VMEM((TABLE_ROWS + 8, BLOCK), jnp.float32)
    hbm = pl.BlockSpec(memory_space=pl.ANY)
    vmem = pl.BlockSpec(memory_space=pltpu.VMEM)
    moved, placed = pl.pallas_call(
        kernel,
        out_shape=(pltpu.VMEM((6, bodies), jnp.float32), pltpu.VMEM((3, bodies), jnp.float32)),
        in_specs=[hbm] * 13,
        out_specs=(vmem, vmem),
        scratch_shapes=[
            pltpu.VMEM((3, bodies), jnp.float32),
            pltpu.VMEM((BLK, BLOCK), jnp.float32),
            pltpu.VMEM((3, bodies), jnp.float32),
            pltpu.VMEM((11, K, bodies), jnp.float32),
            pltpu.VMEM((PLANES, K, bodies), jnp.float32),
            pltpu.VMEM((K, bodies), jnp.int32),
            pltpu.VMEM((K, bodies), jnp.int32),
            pltpu.VMEM((BLK, BLOCK), jnp.int32),
            pltpu.VMEM((2, BLK * 8, BLOCK), jnp.float32),
            pltpu.VMEM((6, bodies), jnp.float32),
            table, table, table,
            pltpu.VMEM((ITERS, 6 * FACE_ROWS, BLOCK), jnp.float32),
            pltpu.VMEM((LAST_GROUP * 72 + 16, BLOCK), jnp.float32),
            pltpu.VMEM((LAST_GROUP * 48, BLOCK), jnp.float32),
            pltpu.VMEM((K, BLK), jnp.int32),
            pltpu.SMEM((6, GHOST), jnp.int32),
            pltpu.VMEM((8, BLK), jnp.int32),
            pltpu.VMEM((32, BLK), jnp.int32),
            pltpu.SMEM((32, BLK), jnp.int32),
            pltpu.SMEM((BLK,), jnp.int32),
            pltpu.SMEM((6 * GHOST,), jnp.int32),
            pltpu.SMEM((BLK,), jnp.int32),
            pltpu.SMEM((BLK * K,), jnp.int32),
            pltpu.SemaphoreType.DMA((13,)),
            pltpu.SemaphoreType.DMA((ITERS, 6)),
            pltpu.SemaphoreType.DMA((ITERS, 6)),
        ],
        compiler_params=pltpu.CompilerParams(collective_id=0, has_side_effects=True),
    )(
        velocity, positions, inverse_mass.reshape(BLK, BLOCK), inverse_inertia, normals, lever_own, lever_other,
        speed_bias, contact_mass, partner_block, partner_lane, slot_counts.reshape(BLK, BLOCK), ghost_blocks,
    )
    return pl.pallas_call(
        finish,
        out_shape=(
            jax.ShapeDtypeStruct((6, bodies), jnp.float32),
            jax.ShapeDtypeStruct((3, bodies), jnp.float32),
        ),
        in_specs=[vmem, vmem],
        out_specs=(hbm, hbm),
        scratch_shapes=[pltpu.SemaphoreType.DMA((2,))],
    )(pltpu.with_memory_space_constraint(moved, pltpu.VMEM), pltpu.with_memory_space_constraint(placed, pltpu.VMEM))


def solution(mesh):
    every = ("gx", "gy", "gz")
    flat, wide, deep = P(every), P(None, every), P(None, None, every)
    return jax.shard_map(
        per_device,
        mesh=mesh,
        in_specs=(wide, wide, flat, wide, deep, deep, deep, wide, wide, wide, wide, flat, wide),
        out_specs=(wide, wide),
        check_vma=False,
    )
```
